32 devices in a mesh: ctx: 8 (over z, x), head: 4 (over y, core).
Axes of the slice: x: 2, y: 2, z: 4, core: 2. Of those that a mesh axis runs over, the one named last changes fastest.
Arguments:
- qkv: bfloat16 [4096, 12288], P(('ctx', 'head')), may hold values from -26 to 26
- grad_out: bfloat16 [4096, 4096], P(('ctx', 'head')), may hold values from -6 to 6
- key_lists: int32 [32, 4], P('ctx'), may hold values from 0 to 31, as said below
- live_counts: int32 [32], P('ctx'), may hold values from 1 to 4
Outputs:
- grad_qkv: bfloat16 [4096, 12288], P(('ctx', 'head'))
The draws below stay inside these ranges and needn't reach their ends.
Inputs may be any that keep to these rules, and one draw needn't show every extreme that they name: `key_lists`: each entry names a block whose index of ctx is within 2 of its query block's and which is not within one block of its query block; the 4 entries of a row differ. Over all 4 entries of all rows (live or not) of one index of ctx, the blocks named on any other index of ctx are at most 2 of its blocks, and this is reached.
All inputs are finite; a program needn't handle non-finite values.
Results may differ from the reference program's by a relative error of at most 0.008.
Values may be sent and summed in bfloat16 or wider, within the bound.
A program may use at most 192 MiB of HBM per device.

```python
import jax
import jax.numpy as jnp
from jax import lax

HEADS = 32
HD = 128
BLK = 128
SEARCHER_TILES = 4
DRAWN_TARGET_SET = 4
SPAN = 2
NAMED_TILE_LIMIT = 2
NB = 32
TOKENS = 4096


def draw_qkv(key, part):
    shape = (TOKENS, HEADS, 3, HD)
    base = jnp.clip(jax.random.normal(key, shape, jnp.float32), -6.0, 6.0)
    return base.reshape(TOKENS, HEADS * 3 * HD).astype(jnp.bfloat16)


def draw_key_lists(key, part):
    shard_total = NB // SEARCHER_TILES
    neighbourhood_halfwidth = 2 * SPAN
    sides = jnp.array([side for side in range(-SPAN, SPAN + 1) if side != 0], dtype=jnp.int32)

    def pick_allowed(subkey):
        return jax.random.permutation(subkey, SEARCHER_TILES)[:NAMED_TILE_LIMIT].astype(jnp.int32)
    allowed = jax.vmap(pick_allowed)(jax.random.split(jax.random.fold_in(key, 11), shard_total * neighbourhood_halfwidth))
    allowed = allowed.reshape(shard_total, neighbourhood_halfwidth, NAMED_TILE_LIMIT)
    tile_ordinals = jnp.arange(NB, dtype=jnp.int32)
    shard_of = tile_ordinals // SEARCHER_TILES
    own_blocks = shard_of[:, None] * SEARCHER_TILES + jnp.arange(SEARCHER_TILES, dtype=jnp.int32)[None, :]
    neighbour = shard_of[:, None] + sides[None, :]
    picked = allowed[shard_of]
    far_blocks = (neighbour[:, :, None] * SEARCHER_TILES + picked).reshape(NB, neighbourhood_halfwidth * NAMED_TILE_LIMIT)
    far_ok = jnp.repeat((neighbour >= 0) & (neighbour < shard_total), NAMED_TILE_LIMIT, axis=1)
    candidates = jnp.concatenate([own_blocks, far_blocks], axis=1)
    usable = jnp.concatenate([jnp.ones((NB, SEARCHER_TILES), bool), far_ok], axis=1)
    usable = usable & (jnp.abs(candidates - tile_ordinals[:, None]) > 1)
    width_all = SEARCHER_TILES + neighbourhood_halfwidth * NAMED_TILE_LIMIT

    def row_order(subkey):
        return jax.random.permutation(subkey, width_all).astype(jnp.int32)
    orders = jax.vmap(row_order)(jax.random.split(jax.random.fold_in(key, 13), NB)) + 1
    tile_merits = jnp.where(usable, orders, 0)
    target_positions = jnp.arange(width_all, dtype=jnp.int32)
    preference_reward = jnp.where((tile_ordinals[:, None] == 0) & (target_positions[None, :] >= SEARCHER_TILES + (neighbourhood_halfwidth - 1) * NAMED_TILE_LIMIT), 1000, 0)
    sorted_tiles = lax.top_k(tile_merits + preference_reward, DRAWN_TARGET_SET)[1]
    return jnp.take_along_axis(candidates, sorted_tiles, axis=1).astype(jnp.int32)


def touch_ends(values, key, low, top_value):
    longest = values.shape.index(max(values.shape))
    spots = []
    for shift in (0, 1):
        where = [jax.random.randint(jax.random.fold_in(key, axis), (), 0, length) for axis, length in enumerate(values.shape)]
        where[longest] = (where[longest] + shift) % values.shape[longest]
        spots.append(tuple(where))
    return values.at[spots[0]].set(low).at[spots[1]].set(top_value)


def block_scale(own_key, dims, cuts, smallest, high):
    gain, own = 1.0, jax.random.fold_in(own_key, 6)
    for position, parts in cuts:
        steps = jnp.exp(jax.random.uniform(jax.random.fold_in(own, position), (parts,), jnp.float32, smallest / len(cuts), high / len(cuts)))
        gain = gain * jnp.repeat(steps, dims[position] // parts).reshape([-1 if axis == position else 1 for axis in range(len(dims))])
    return gain


def noise(key, dims, scale, reach, cuts=(), held_as=jnp.bfloat16):
    values = jax.random.normal(key, dims, jnp.float32) * scale
    if len(cuts) > 0:
        values = block_scale(key, dims, cuts, -0.22, 0.18) * values
    return jnp.clip(values, min=-reach, max=reach).astype(held_as)


def setup_inputs(seed: int = 0) -> dict:
    arg_keys = jax.random.split(jax.random.key(seed), 5)
    qkv = draw_qkv(jax.random.fold_in(arg_keys[4], 71), 0)
    grad_out = noise(arg_keys[1], (TOKENS, HEADS * HD), 1.0, 6.0, ((0, 32),))
    key_lists = draw_key_lists(jax.random.fold_in(arg_keys[4], 71), 0)
    live_counts = touch_ends(jax.random.randint(arg_keys[3], (NB,), 1, DRAWN_TARGET_SET + 1), jax.random.fold_in(arg_keys[3], 1), 1, DRAWN_TARGET_SET).astype(jnp.int32)
    return {"qkv": qkv, "grad_out": grad_out, "key_lists": key_lists, "live_counts": live_counts}


def reference(qkv, grad_out, key_lists, live_counts):
    total_blocks = key_lists.shape[0]
    scaling = HD ** -0.5
    merged = qkv.reshape(total_blocks, BLK, HEADS, 3, HD)
    queries = merged[:, :, :, 0]
    key_rows = merged[:, :, :, 1]
    value_rows = merged[:, :, :, 2]
    grads_in = grad_out.reshape(total_blocks, BLK, HEADS, HD)

    def one_block(totals, block_id):
        window = block_id - 1 + jnp.arange(3, dtype=jnp.int32)
        listed = key_lists[block_id].astype(jnp.int32)
        named = jnp.concatenate([window, listed]).astype(jnp.int32)
        usable = jnp.concatenate([(window >= 0) & (window < total_blocks), jnp.arange(DRAWN_TARGET_SET, dtype=jnp.int32) < live_counts[block_id]])
        clipped = jnp.clip(named, 0, total_blocks - 1).astype(jnp.int32)
        key_part = key_rows[clipped].astype(jnp.float32)
        value_part = value_rows[clipped].astype(jnp.float32)
        query_part = queries[block_id].astype(jnp.float32)
        grad_part = grads_in[block_id].astype(jnp.float32)
        weight = usable.astype(jnp.float32)[None, None, :, None]
        tile_merits = jnp.einsum("qhd,nkhd->hqnk", query_part, key_part) * scaling
        masked = jnp.where(weight > 0.0, tile_merits, -1.0e30)
        highest = jnp.max(masked, axis=(2, 3), keepdims=True)
        powers = jnp.exp(masked - highest) * weight
        soft_weights = powers / jnp.sum(powers, axis=(2, 3), keepdims=True)
        grad_soft = jnp.einsum("qhd,nkhd->hqnk", grad_part, value_part)
        row_delta = jnp.sum(soft_weights * grad_soft, axis=(2, 3), keepdims=True)
        grad_scores = soft_weights * (grad_soft - row_delta)
        soft_low = soft_weights.astype(jnp.bfloat16).astype(jnp.float32)
        scores_low = grad_scores.astype(jnp.bfloat16).astype(jnp.float32)
        grad_values = jnp.einsum("hqnk,qhd->nkhd", soft_low, grad_part)
        grad_keys = jnp.einsum("hqnk,qhd->nkhd", scores_low, query_part) * scaling
        grad_query = jnp.einsum("hqnk,nkhd->qhd", scores_low, key_part) * scaling
        totals = totals.at[clipped].add(jnp.stack([grad_keys, grad_values], axis=3))
        return totals, grad_query

    start_totals = jnp.zeros((total_blocks, BLK, HEADS, 2, HD), jnp.float32)
    totals, grad_query = lax.scan(one_block, start_totals, jnp.arange(total_blocks, dtype=jnp.int32))
    joined = jnp.concatenate([grad_query[:, :, :, None, :], totals], axis=3)
    return joined.astype(jnp.bfloat16).reshape(total_blocks * BLK, HEADS * 3 * HD)
```

```python
import functools

import jax
import jax.numpy as jnp
from jax import lax
from jax.experimental import pallas as pl
from jax.experimental.pallas import tpu as pltpu
from jax.sharding import Mesh, PartitionSpec as P

HD = 128
BLK = 128
TILES = 4
LISTED = 4
NAMED = 2
PAIR = 2 * TILES
EDGE = NAMED + TILES
ALL = 2 * EDGE + PAIR
SCALE = HD ** (-0.5)
MESH = pl.DeviceIdType.MESH
I32 = jnp.int32
F32 = jnp.float32
BF16 = jnp.bfloat16


def rows(block, count=1):
    start = block * BLK
    return pl.ds(start if isinstance(start, int) else pl.multiple_of(start, BLK), count * BLK)


def position(sizes):
    pairs_total, heads_total, ways = sizes
    z = lax.axis_index("cz")
    me = lax.axis_index("cx") * heads_total + lax.axis_index("head")
    return z, me


def peer_id(peer, sizes):
    return {"cx": peer // sizes[1], "head": peer % sizes[1]}


def greet(sizes):
    pairs_total, _, ways = sizes
    z, me = position(sizes)
    x = lax.axis_index("cx")
    side = z - 1 + 2 * x
    inside = (side >= 0) & (side < pairs_total)
    barrier = pltpu.get_barrier_semaphore()

    def signal(device_id):
        pl.semaphore_signal(barrier, inc=1, device_id=device_id, device_id_type=MESH)

    for k in range(1, ways):
        signal(peer_id((me + k) % ways, sizes))
    pl.when(z > 0)(lambda: signal({"cz": z - 1}))
    pl.when(z < pairs_total - 1)(lambda: signal({"cz": z + 1}))
    pl.when(inside)(lambda: signal({"cz": side, "cx": 1 - x}))
    neighbours = jnp.minimum(z, 1) + jnp.minimum(pairs_total - 1 - z, 1) + jnp.where(inside, 1, 0)
    pl.semaphore_wait(barrier, ways - 1 + neighbours)


def remote(src, dst, send, recv, device_id):
    return pltpu.make_async_remote_copy(
        src_ref=src, dst_ref=dst, send_sem=send, recv_sem=recv, device_id=device_id, device_id_type=MESH
    )


def pack(lists, key_lists, live_counts, pairs_total, z, x):
    row = lax.broadcasted_iota(I32, (8, 128), 0)
    col = lax.broadcasted_iota(I32, (8, 128), 1)
    value = jnp.full((8, 128), -1, I32)
    for b in range(TILES):
        for j in range(LISTED):
            value = jnp.where((row == b) & (col == j), key_lists[b, j], value)
        value = jnp.where((row == b) & (col == LISTED), live_counts[b], value)
    lists[x] = value

    @pl.when(z == pairs_total - 1)
    def _():
        lists[2] = jnp.full((8, 128), -1, I32)

    @pl.when(z == 0)
    def _():
        lists[3] = jnp.full((8, 128), -1, I32)


def tables(tab, places, slots, chains, z):
    base = z * PAIR

    def named(run, first):
        flags = [jnp.int32(0)] * TILES
        for b in range(TILES):
            for j in range(LISTED):
                at = tab[run, b, j] - first
                flags = [jnp.where(at == t, 1, flag) for t, flag in enumerate(flags)]
        ranks = [jnp.int32(0)]
        for flag in flags[:-1]:
            ranks.append(ranks[-1] + flag)
        return flags, ranks

    for side, (run, first) in enumerate(((2, base), (3, base + TILES))):
        flags, ranks = named(run, first)
        for s in range(NAMED):
            chosen = jnp.int32(0)
            for t in range(TILES):
                chosen = jnp.where((flags[t] == 1) & (ranks[t] == s), t, chosen)
            slots[side, s] = chosen
    row = lax.broadcasted_iota(I32, (8, 128), 0)
    col = lax.broadcasted_iota(I32, (8, 128), 1)
    before = jnp.zeros((8, 128), I32)
    last = jnp.zeros((8, 128), I32)
    along = jnp.full((8, 128), -1, I32)
    found = []
    for run, (first, start) in enumerate(((base - PAIR, 0), (base + PAIR + TILES, EDGE + PAIR + TILES))):
        _, ranks = named(run, first)
        for b in range(TILES):
            for j in range(LISTED):
                block = tab[run, b, j]
                far = jnp.int32(0)
                for t in range(1, TILES):
                    far = jnp.where(block - first == t, ranks[t], far)
                outside = (block < base - TILES) if run == 0 else (block >= base + PAIR + TILES)
                place = jnp.where(outside, start + far, EDGE + block - base)
                place = jnp.clip(place, 0, ALL - 1)
                places[run * TILES + b, j] = place
                found.append(place)
    for n, place in enumerate(found):
        along = jnp.where(col == n, place, along)
    for n, place in enumerate(found):
        before = jnp.where((along == place) & (col > n), n + 1, before)
        last = jnp.where(col == place, n + 1, last)
    chains[...] = jnp.where(row == 0, before, last)


def layer_kernel(
    sizes, key_lists, live_counts, qkv, grads, out,
    own, left, right, stage, pairs, acc, chain, own_grads, left_grads, right_grads, from_next, from_prev, joined,
    lists, chains, tab, links, places, slots,
    send, recv, local, edge_send, edge_recv, back_edge_send, back_edge_recv, back_send, back_recv, back_local,
    list_send, list_recv, table_sem,
):
    pairs_total, _, ways = sizes
    heads = own.shape[0]
    z, me = position(sizes)
    x = lax.axis_index("cx")
    wide, slim = 3 * HD, HD
    inner = (z > 0, z < pairs_total - 1)
    kv = pl.ds(HD, 2 * HD)
    pack(lists, key_lists, live_counts, pairs_total, z, x)
    greet(sizes)

    def piece(h, device, block, t):
        at = device * heads + h
        start = pl.multiple_of(at * wide, HD)
        if t == 0:
            return qkv.at[:, pl.ds(start + HD, 2 * HD)], own.at[h, rows(block), kv]
        if t == 1:
            return qkv.at[:, pl.ds(start, HD)], own.at[h, rows(block), pl.ds(0, HD)]
        return grads.at[:, pl.ds(pl.multiple_of(at * slim, HD), slim)], own.at[h, rows(block), pl.ds(wide, slim)]

    side = z - 1 + 2 * x
    beyond = (side >= 0) & (side < pairs_total)
    list_other = remote(lists.at[x], lists.at[x], list_send.at[0], list_recv.at[0], {"cx": 1 - x})
    list_side = [
        remote(lists.at[x], lists.at[2 + x], list_send.at[1], list_recv.at[1 + x], {"cz": side}),
        remote(lists.at[x], lists.at[2 + x], list_send.at[2], list_recv.at[1 + x], {"cz": side, "cx": 1 - x}),
    ]
    list_other.start()
    pl.when(beyond)(lambda: [c.start() for c in list_side] and None)

    sends = []

    def fetch(h, kinds):
        for k in range(1, ways):
            peer = (me + k) % ways
            for t in kinds:
                src, dst = piece(h, peer, me, t)
                copy = remote(src, dst, send.at[h, k, t], recv.at[h, k, t], peer_id(peer, sizes))
                copy.start()
                sends.append(copy)
        for t in kinds:
            src, dst = piece(h, me, me, t)
            pltpu.make_async_copy(src, dst, local.at[h, t]).start()

    def arrived(h, kinds):
        for t in kinds:
            for k in range(1, ways):
                source = (me + ways - k) % ways
                src, dst = piece(h, source, source, t)
                remote(src, dst, send.at[h, k, t], recv.at[h, k, t], peer_id(source, sizes)).wait_recv()
            src, dst = piece(h, me, me, t)
            pltpu.make_async_copy(src, dst, local.at[h, t]).wait()

    ahead = [("kv", 0), ("rest", 0), ("kv", 1)]
    for h in range(2, heads):
        ahead += [("kv", h), ("rest", h - 1)]
    ahead += [("rest", heads - 1)] if heads > 1 else []
    for kind, h in ahead:
        if h < heads:
            fetch(h, (0,) if kind == "kv" else (1, 2))

    @pl.when(z == 0)
    def _():
        left[...] = jnp.zeros_like(left)
        from_prev[...] = jnp.zeros_like(from_prev)

    @pl.when(z == pairs_total - 1)
    def _():
        right[...] = jnp.zeros_like(right)
        from_next[...] = jnp.zeros_like(from_next)

    chain[0] = jnp.zeros((BLK, 2 * HD), F32)

    list_other_in = remote(lists.at[1 - x], lists.at[1 - x], list_send.at[0], list_recv.at[0], {"cx": 1 - x})
    list_other_in.wait_recv()
    for n, there in ((0, inner[1]), (1, inner[0])):
        come = remote(lists.at[2 + n], lists.at[2 + n], list_send.at[1], list_recv.at[1 + n], {"cx": 1 - x})
        pl.when(there)(come.wait_recv)
    copy = pltpu.make_async_copy(lists, tab, table_sem.at[0])
    copy.start()
    copy.wait()
    tables(tab, places, slots, chains, z)
    copy = pltpu.make_async_copy(chains, links, table_sem.at[1])
    copy.start()
    copy.wait()

    def edge_copies(h):
        up = [
            remote(src, left.at[h, part], edge_send.at[h, 0, n], edge_recv.at[h, 0, n], {"cz": z + 1})
            for n, (src, part) in enumerate(
                ((stage.at[h, 0], rows(0, NAMED)), (own.at[h, rows(TILES, TILES), kv], rows(NAMED, TILES)))
            )
        ]
        down = [
            remote(src, right.at[h, part], edge_send.at[h, 1, n], edge_recv.at[h, 1, n], {"cz": z - 1})
            for n, (src, part) in enumerate(
                ((stage.at[h, 1], rows(TILES, NAMED)), (own.at[h, rows(0, TILES), kv], rows(0, TILES)))
            )
        ]
        return up, down

    def back_edge_copies(h):
        up = remote(right_grads.at[h], from_prev.at[h], back_edge_send.at[h, 0], back_edge_recv.at[h, 0], {"cz": z + 1})
        down = remote(left_grads.at[h], from_next.at[h], back_edge_send.at[h, 1], back_edge_recv.at[h, 1], {"cz": z - 1})
        return [up], [down]

    def start(copies):
        up, down = copies
        pl.when(inner[1])(lambda: [c.start() for c in up] and None)
        pl.when(inner[0])(lambda: [c.start() for c in down] and None)

    def arrive(copies):
        up, down = copies
        pl.when(inner[0])(lambda: [c.wait_recv() for c in up] and None)
        pl.when(inner[1])(lambda: [c.wait_recv() for c in down] and None)

    def leave(copies):
        up, down = copies
        pl.when(inner[1])(lambda: [c.wait_send() for c in up] and None)
        pl.when(inner[0])(lambda: [c.wait_send() for c in down] and None)

    def edges(h):
        arrived(h, (0,))
        for s in range(NAMED):
            for side in range(2):
                chosen = own[h, rows(side * TILES), HD : 3 * HD]
                for t in range(1, TILES):
                    chosen = jnp.where(slots[side, s] == t, own[h, rows(side * TILES + t), HD : 3 * HD], chosen)
                stage[h, side, rows(s), :] = chosen
        start(edge_copies(h))

    def attend(h, middle):
        arrived(h, (1, 2))
        arrive(edge_copies(h))
        pairs[:EDGE] = left[h].reshape(EDGE, BLK, 2 * HD)
        pairs[EDGE : EDGE + PAIR] = own[h, :, HD : 3 * HD].reshape(PAIR, BLK, 2 * HD)
        pairs[EDGE + PAIR :] = right[h].reshape(EDGE, BLK, 2 * HD)
        acc[...] = jnp.zeros_like(acc)

        def step(i, carry):
            q = own[h, rows(i), :HD]
            g = own[h, rows(i), 3 * HD :]
            zero = jnp.zeros_like(q)
            both = jnp.concatenate(
                [jnp.concatenate([q, zero], axis=1), jnp.concatenate([zero, g], axis=1)], axis=0
            )
            block = z * PAIR + i
            live = tab[i // TILES, i % TILES, LISTED]
            usable = [block > 0, None, block < pairs_total * PAIR - 1] + [live > j for j in range(LISTED)]
            kv = jnp.concatenate(
                [pairs[EDGE - 1 + i + n] for n in range(3)] + [pairs[places[i, j]] for j in range(LISTED)], axis=0
            )
            products = lax.dot_general(kv, both, (((1,), (1,)), ((), ())), preferred_element_type=F32)
            scores = []
            for n, ok in enumerate(usable):
                s = products[n * BLK : (n + 1) * BLK, :HD] * SCALE
                scores.append(s if ok is None else jnp.where(ok, s, -1e30))
            scores = jnp.concatenate(scores, axis=0)
            powers = jnp.exp(scores - jnp.max(scores, axis=0, keepdims=True))
            soft = powers * (1.0 / jnp.sum(powers, axis=0, keepdims=True))
            dp = products[:, HD:]
            ds = soft * (dp - jnp.sum(soft * dp, axis=0, keepdims=True))
            ds_low = ds.astype(BF16)
            low = jnp.concatenate([ds_low, soft.astype(BF16)], axis=1)
            terms = jnp.dot(low, both, preferred_element_type=F32)
            grad_q = lax.dot_general(ds_low, kv[:, :HD], (((0,), (0,)), ((), ())), preferred_element_type=F32)
            joined[h, rows(i), :HD] = (grad_q * SCALE).astype(BF16)
            acc[rows(EDGE - 1 + i, 3), :] += terms[: 3 * BLK]
            for j in range(LISTED):
                n = i * LISTED + j
                chain[n + 1] = terms[(3 + j) * BLK : (4 + j) * BLK] + chain[links[0, n]]
            return carry

        lax.fori_loop(0, PAIR // 2, step, 0)
        middle()
        lax.fori_loop(PAIR // 2, PAIR, step, 0)

        def total(p):
            value = acc[rows(p), :] + chain[links[1, p]]
            return jnp.concatenate([value[:, :HD] * SCALE, value[:, HD:]], axis=1)

        def edge_total(p, carry):
            left_grads[h, rows(p), :] = total(p).astype(BF16)
            right_grads[h, rows(p), :] = total(EDGE + PAIR + p).astype(BF16)
            return carry

        def own_total(p, carry):
            own_grads[h, rows(p), :] = total(EDGE + p)
            return carry

        lax.fori_loop(0, EDGE, edge_total, 0)
        start(back_edge_copies(h))
        lax.fori_loop(0, PAIR, own_total, 0)

    back_sends, back_locals = [], []
    parts = (slice(0, HD), slice(HD, 3 * HD))

    def column(device, h, t):
        first = pl.multiple_of((device * heads + h) * wide, HD)
        return out.at[:, pl.ds(first, HD)] if t == 0 else out.at[:, pl.ds(first + HD, 2 * HD)]

    def give(h, t):
        for k in range(1, ways):
            peer = (me + k) % ways
            copy = remote(
                joined.at[h, rows(peer), parts[t]], column(me, h, t), back_send.at[h, k, t], back_recv.at[h, k, t],
                peer_id(peer, sizes),
            )
            copy.start()
            back_sends.append(copy)
        copy = pltpu.make_async_copy(joined.at[h, rows(me), parts[t]], column(me, h, t), back_local.at[h, t])
        copy.start()
        back_locals.append(copy)

    def combine(h):
        arrive(back_edge_copies(h))
        for t in range(PAIR):
            value = own_grads[h, rows(t), :]
            if t < TILES:
                near, far, table, base = from_prev, from_next, 0, t
                near_at, far_at = t, 0
            else:
                near, far, table, base = from_next, from_prev, 1, t - TILES
                near_at, far_at = NAMED + t - TILES, TILES
            value += near[h, rows(near_at), :].astype(F32)
            for s in range(NAMED):
                term = far[h, rows(far_at + s), :].astype(F32)
                value += jnp.where(slots[table, s] == base, term, 0.0)
            joined[h, rows(t), HD:] = value.astype(BF16)
        give(h, 1)

    edges(0)
    for h in range(heads):
        attend(h, functools.partial(edges, h + 1) if h + 1 < heads else lambda: None)
        give(h, 0)
        if h > 0:
            combine(h - 1)
    combine(heads - 1)

    for h in range(heads):
        for t in range(2):
            for k in range(1, ways):
                source = (me + ways - k) % ways
                remote(
                    joined.at[h, rows(source), parts[t]], column(source, h, t), back_send.at[h, k, t],
                    back_recv.at[h, k, t], peer_id(source, sizes),
                ).wait_recv()
        leave(edge_copies(h))
        leave(back_edge_copies(h))
    for copy in back_locals:
        copy.wait()
    for copy in sends + back_sends:
        copy.wait_send()
    list_other.wait_send()
    pl.when(beyond)(lambda: [c.wait_send() for c in list_side] and None)


def shards(qkv, grad_out, key_lists, live_counts):
    heads_total = lax.axis_size("head")
    ways = lax.axis_size("cx") * heads_total
    sizes = (lax.axis_size("cz"), heads_total, ways)
    heads = qkv.shape[1] // (3 * HD) // ways
    full = qkv.shape[0] * ways
    smem = pl.BlockSpec(memory_space=pltpu.SMEM)
    hbm = pl.BlockSpec(memory_space=pltpu.HBM)
    dma = pltpu.SemaphoreType.DMA
    edge = pltpu.VMEM((heads, EDGE * BLK, 2 * HD), BF16)
    return pl.pallas_call(
        functools.partial(layer_kernel, sizes),
        in_specs=[smem, smem, hbm, hbm],
        out_specs=pl.BlockSpec(memory_space=pltpu.VMEM),
        out_shape=pltpu.VMEM(qkv.shape, BF16),
        scratch_shapes=[
            pltpu.VMEM((heads, full, 4 * HD), BF16), edge, edge,
            pltpu.VMEM((heads, 2, NAMED * BLK, 2 * HD), BF16),
            pltpu.VMEM((ALL, BLK, 2 * HD), BF16),
            pltpu.VMEM((ALL * BLK, 2 * HD), F32),
            pltpu.VMEM((PAIR * LISTED + 1, BLK, 2 * HD), F32),
            pltpu.VMEM((heads, full, 2 * HD), F32),
            edge, edge, edge, edge,
            pltpu.VMEM((heads, full, 3 * HD), BF16),
            pltpu.VMEM((4, 8, 128), I32), pltpu.VMEM((8, 128), I32),
            pltpu.SMEM((4, 8, 128), I32), pltpu.SMEM((8, 128), I32),
            pltpu.SMEM((PAIR, LISTED), I32), pltpu.SMEM((2, NAMED), I32),
            dma((heads, ways, 3)), dma((heads, ways, 3)), dma((heads, 3)),
            dma((heads, 2, 2)), dma((heads, 2, 2)), dma((heads, 2)), dma((heads, 2)),
            dma((heads, ways, 2)), dma((heads, ways, 2)), dma((heads, 2)),
            dma((3,)), dma((3,)), dma((2,)),
        ],
        compiler_params=pltpu.CompilerParams(
            collective_id=0, has_side_effects=True, vmem_limit_bytes=60_000_000
        ),
        name="layer",
    )(key_lists, live_counts, qkv, grad_out)


def solution(mesh):
    ctx, head = mesh.shape["ctx"], mesh.shape["head"]
    split = Mesh(mesh.devices.reshape(ctx // 2, 2, head), ("cz", "cx", "head"))
    both = ("cz", "cx")
    tokens = P((*both, "head"), None)
    return jax.shard_map(
        shards, mesh=split, in_specs=(tokens, tokens, P(both, None), P(both)), out_specs=tokens, check_vma=False
    )
```

```python
import functools

import jax
import jax.numpy as jnp
from jax import lax
from jax.experimental import pallas as pl
from jax.experimental.pallas import tpu as pltpu
from jax.sharding import Mesh, PartitionSpec as P

HD = 128
BLK = 128
TILES = 4
LISTED = 4
NAMED = 2
PAIR = 2 * TILES
EDGE = NAMED + TILES
ALL = 2 * EDGE + PAIR
WIDTH = 3 + LISTED
AHEAD = 1
MIDDLE = 4
SCALE = HD ** (-0.5)
RATE = SCALE * 1.4426950408889634
MESH = pl.DeviceIdType.MESH
I32 = jnp.int32
F32 = jnp.float32
BF16 = jnp.bfloat16


def rows(block, count=1):
    start = block * BLK
    return pl.ds(start if isinstance(start, int) else pl.multiple_of(start, BLK), count * BLK)


def position(sizes):
    pairs_total, heads_total, ways = sizes
    z = lax.axis_index("cz")
    me = lax.axis_index("cx") * heads_total + lax.axis_index("head")
    return z, me


def peer_id(peer, sizes):
    return {"cx": peer // sizes[1], "head": peer % sizes[1]}


def greet(sizes):
    pairs_total, _, ways = sizes
    z, me = position(sizes)
    x = lax.axis_index("cx")
    side = z - 1 + 2 * x
    inside = (side >= 0) & (side < pairs_total)
    barrier = pltpu.get_barrier_semaphore()

    def signal(device_id):
        pl.semaphore_signal(barrier, inc=1, device_id=device_id, device_id_type=MESH)

    for k in range(1, ways):
        signal(peer_id((me + k) % ways, sizes))
    pl.when(z > 0)(lambda: signal({"cz": z - 1}))
    pl.when(z < pairs_total - 1)(lambda: signal({"cz": z + 1}))
    pl.when(inside)(lambda: signal({"cz": side, "cx": 1 - x}))
    neighbours = jnp.minimum(z, 1) + jnp.minimum(pairs_total - 1 - z, 1) + jnp.where(inside, 1, 0)
    pl.semaphore_wait(barrier, ways - 1 + neighbours)


def remote(src, dst, send, recv, device_id):
    return pltpu.make_async_remote_copy(
        src_ref=src, dst_ref=dst, send_sem=send, recv_sem=recv, device_id=device_id, device_id_type=MESH
    )


def pack(lists, key_lists, live_counts, pairs_total, z, x):
    row = lax.broadcasted_iota(I32, (8, 128), 0)
    col = lax.broadcasted_iota(I32, (8, 128), 1)
    value = jnp.full((8, 128), -1, I32)
    for b in range(TILES):
        for j in range(LISTED):
            value = jnp.where((row == b) & (col == j), key_lists[b, j], value)
        value = jnp.where((row == b) & (col == LISTED), live_counts[b], value)
    lists[x] = value

    @pl.when(z == pairs_total - 1)
    def _():
        lists[2] = jnp.full((8, 128), -1, I32)

    @pl.when(z == 0)
    def _():
        lists[3] = jnp.full((8, 128), -1, I32)


def tables(tab, places, slots, chains, z):
    base = z * PAIR

    def named(run, first):
        flags = [jnp.int32(0)] * TILES
        for b in range(TILES):
            for j in range(LISTED):
                at = tab[run, b, j] - first
                flags = [jnp.where(at == t, 1, flag) for t, flag in enumerate(flags)]
        ranks = [jnp.int32(0)]
        for flag in flags[:-1]:
            ranks.append(ranks[-1] + flag)
        return flags, ranks

    for side, (run, first) in enumerate(((2, base), (3, base + TILES))):
        flags, ranks = named(run, first)
        for s in range(NAMED):
            chosen = jnp.int32(0)
            for t in range(TILES):
                chosen = jnp.where((flags[t] == 1) & (ranks[t] == s), t, chosen)
            slots[side, s] = chosen
    row = lax.broadcasted_iota(I32, (8, 128), 0)
    col = lax.broadcasted_iota(I32, (8, 128), 1)
    before = jnp.zeros((8, 128), I32)
    last = jnp.zeros((8, 128), I32)
    along = jnp.full((8, 128), -1, I32)
    found = []
    for run, (first, start) in enumerate(((base - PAIR, 0), (base + PAIR + TILES, EDGE + PAIR + TILES))):
        _, ranks = named(run, first)
        for b in range(TILES):
            for j in range(LISTED):
                block = tab[run, b, j]
                far = jnp.int32(0)
                for t in range(1, TILES):
                    far = jnp.where(block - first == t, ranks[t], far)
                outside = (block < base - TILES) if run == 0 else (block >= base + PAIR + TILES)
                place = jnp.where(outside, start + far, EDGE + block - base)
                place = jnp.clip(place, 0, ALL - 1)
                places[run * TILES + b, j] = place
                found.append(place)
    for n, place in enumerate(found):
        along = jnp.where(col == n, place, along)
    for n, place in enumerate(found):
        before = jnp.where((along == place) & (col > n), n + 1, before)
        last = jnp.where(col == place, n + 1, last)
    chains[...] = jnp.where(row == 0, before, last)


def layer_kernel(
    sizes, key_lists, live_counts, qkv, grads, out,
    own, left, right, stage, pairs, acc, chain, even, odd, own_grads, left_grads, right_grads, from_next, from_prev, joined,
    lists, chains, tab, links, places, slots,
    send, recv, local, edge_send, edge_recv, back_edge_send, back_edge_recv, back_send, back_recv, back_local,
    list_send, list_recv, table_sem,
):
    pairs_total, _, ways = sizes
    heads = own.shape[0]
    z, me = position(sizes)
    x = lax.axis_index("cx")
    wide, slim = 3 * HD, HD
    inner = (z > 0, z < pairs_total - 1)
    kv = pl.ds(HD, 2 * HD)
    pack(lists, key_lists, live_counts, pairs_total, z, x)
    greet(sizes)

    def piece(h, device, block, t):
        at = device * heads + h
        start = pl.multiple_of(at * wide, HD)
        if t == 0:
            return qkv.at[:, pl.ds(start + HD, 2 * HD)], own.at[h, rows(block), kv]
        if t == 1:
            return qkv.at[:, pl.ds(start, HD)], own.at[h, rows(block), pl.ds(0, HD)]
        return grads.at[:, pl.ds(pl.multiple_of(at * slim, HD), slim)], own.at[h, rows(block), pl.ds(wide, slim)]

    side = z - 1 + 2 * x
    beyond = (side >= 0) & (side < pairs_total)
    list_other = remote(lists.at[x], lists.at[x], list_send.at[0], list_recv.at[0], {"cx": 1 - x})
    list_side = [
        remote(lists.at[x], lists.at[2 + x], list_send.at[1], list_recv.at[1 + x], {"cz": side}),
        remote(lists.at[x], lists.at[2 + x], list_send.at[2], list_recv.at[1 + x], {"cz": side, "cx": 1 - x}),
    ]
    list_other.start()
    pl.when(beyond)(lambda: [c.start() for c in list_side] and None)

    sends = []

    def fetch(h, kinds):
        for k in range(1, ways):
            peer = (me + k) % ways
            for t in kinds:
                src, dst = piece(h, peer, me, t)
                copy = remote(src, dst, send.at[h, k, t], recv.at[h, k, t], peer_id(peer, sizes))
                copy.start()
                sends.append(copy)
        for t in kinds:
            src, dst = piece(h, me, me, t)
            pltpu.make_async_copy(src, dst, local.at[h, t]).start()

    def arrived(h, kinds):
        for t in kinds:
            for k in range(1, ways):
                source = (me + ways - k) % ways
                src, dst = piece(h, source, source, t)
                remote(src, dst, send.at[h, k, t], recv.at[h, k, t], peer_id(source, sizes)).wait_recv()
            src, dst = piece(h, me, me, t)
            pltpu.make_async_copy(src, dst, local.at[h, t]).wait()

    for h in range(heads + AHEAD):
        if h < heads:
            fetch(h, (0,))
        if h >= AHEAD:
            fetch(h - AHEAD, (1, 2))

    @pl.when(z == 0)
    def _():
        left[...] = jnp.zeros_like(left)
        from_prev[...] = jnp.zeros_like(from_prev)

    @pl.when(z == pairs_total - 1)
    def _():
        right[...] = jnp.zeros_like(right)
        from_next[...] = jnp.zeros_like(from_next)

    chain[0] = jnp.zeros((BLK, 2 * HD), F32)

    list_other_in = remote(lists.at[1 - x], lists.at[1 - x], list_send.at[0], list_recv.at[0], {"cx": 1 - x})
    list_other_in.wait_recv()
    for n, there in ((0, inner[1]), (1, inner[0])):
        come = remote(lists.at[2 + n], lists.at[2 + n], list_send.at[1], list_recv.at[1 + n], {"cx": 1 - x})
        pl.when(there)(come.wait_recv)
    copy = pltpu.make_async_copy(lists, tab, table_sem.at[0])
    copy.start()
    copy.wait()
    tables(tab, places, slots, chains, z)
    copy = pltpu.make_async_copy(chains, links, table_sem.at[1])
    copy.start()
    copy.wait()

    def edge_copies(h):
        up = [
            remote(src, left.at[h, part], edge_send.at[h, 0, n], edge_recv.at[h, 0, n], {"cz": z + 1})
            for n, (src, part) in enumerate(
                ((stage.at[h, 0], rows(0, NAMED)), (own.at[h, rows(TILES, TILES), kv], rows(NAMED, TILES)))
            )
        ]
        down = [
            remote(src, right.at[h, part], edge_send.at[h, 1, n], edge_recv.at[h, 1, n], {"cz": z - 1})
            for n, (src, part) in enumerate(
                ((stage.at[h, 1], rows(TILES, NAMED)), (own.at[h, rows(0, TILES), kv], rows(0, TILES)))
            )
        ]
        return up, down

    def back_edge_copies(h, t):
        part = pl.ds(t * HD, HD)
        up = remote(
            right_grads.at[h, :, part], from_prev.at[h, :, part],
            back_edge_send.at[h, 0, t], back_edge_recv.at[h, 0, t], {"cz": z + 1},
        )
        down = remote(
            left_grads.at[h, :, part], from_next.at[h, :, part],
            back_edge_send.at[h, 1, t], back_edge_recv.at[h, 1, t], {"cz": z - 1},
        )
        return [up], [down]

    def start(copies):
        up, down = copies
        pl.when(inner[1])(lambda: [c.start() for c in up] and None)
        pl.when(inner[0])(lambda: [c.start() for c in down] and None)

    def arrive(copies):
        up, down = copies
        pl.when(inner[0])(lambda: [c.wait_recv() for c in up] and None)
        pl.when(inner[1])(lambda: [c.wait_recv() for c in down] and None)

    def leave(copies):
        up, down = copies
        pl.when(inner[1])(lambda: [c.wait_send() for c in up] and None)
        pl.when(inner[0])(lambda: [c.wait_send() for c in down] and None)

    def edges(h):
        arrived(h, (0,))
        for s in range(NAMED):
            for side in range(2):
                chosen = own[h, rows(side * TILES), HD : 3 * HD]
                for t in range(1, TILES):
                    chosen = jnp.where(slots[side, s] == t, own[h, rows(side * TILES + t), HD : 3 * HD], chosen)
                stage[h, side, rows(s), :] = chosen
        start(edge_copies(h))

    def attend(h, middle=None):
        arrived(h, (1, 2))
        arrive(edge_copies(h))
        pairs[:EDGE] = left[h].reshape(EDGE, BLK, 2 * HD)
        pairs[EDGE : EDGE + PAIR] = own[h, :, HD : 3 * HD].reshape(PAIR, BLK, 2 * HD)
        pairs[EDGE + PAIR :] = right[h].reshape(EDGE, BLK, 2 * HD)
        acc[...] = jnp.zeros_like(acc)

        def operand(i):
            q = own[h, rows(i), :HD]
            g = own[h, rows(i), 3 * HD :]
            zero = jnp.zeros_like(q)
            return jnp.concatenate(
                [jnp.concatenate([q, zero], axis=1), jnp.concatenate([zero, g], axis=1)], axis=0
            )

        def keys(i, columns):
            near = [pairs[EDGE - 1 + i + n, :, columns] for n in range(3)]
            return jnp.concatenate(near + [pairs[places[i, j], :, columns] for j in range(LISTED)], axis=0)

        def issue(i, slot):
            slot[...] = lax.dot_general(
                keys(i, slice(None)), operand(i), (((1,), (1,)), ((), ())), preferred_element_type=F32
            )

        def settle(i, products):
            block = z * PAIR + i
            live = tab[i // TILES, i % TILES, LISTED]
            usable = [block > 0, None, block < pairs_total * PAIR - 1] + [live > j for j in range(LISTED)]
            tiles = [products[n * BLK : (n + 1) * BLK, :HD] for n in range(WIDTH)]
            peaks = [jnp.max(s.reshape(BLK // 8, 8, HD), axis=0) for s in tiles]
            peaks = [s if ok is None else jnp.where(ok, s, -1e30) for s, ok in zip(peaks, usable)]
            shift = jnp.max(functools.reduce(jnp.maximum, peaks), axis=0, keepdims=True) * -RATE
            shifts = [shift if ok is None else jnp.where(ok, shift, -1e30) for ok in usable]
            powers = jnp.concatenate([jnp.exp2(s * RATE + b) for s, b in zip(tiles, shifts)], axis=0)
            dp = products[:, HD:]
            over = 1.0 / jnp.sum(powers, axis=0, keepdims=True)
            soft = powers * over
            ds = soft * (dp - jnp.sum(powers * dp, axis=0, keepdims=True) * over)
            ds_low = ds.astype(BF16)
            low = jnp.concatenate([ds_low, soft.astype(BF16)], axis=1)
            terms = jnp.dot(low, operand(i), preferred_element_type=F32)
            grad_q = lax.dot_general(
                ds_low, keys(i, slice(0, HD)), (((0,), (0,)), ((), ())), preferred_element_type=F32
            )
            joined[h, rows(i), :HD] = (grad_q * SCALE).astype(BF16)
            acc[rows(EDGE - 1 + i, 3), :] += terms[: 3 * BLK]
            for j in range(LISTED):
                n = i * LISTED + j
                chain[n + 1] = terms[(3 + j) * BLK : (4 + j) * BLK] + chain[links[0, n]]

        def step(n, carry):
            i = 2 * n
            issue(i + 1, odd)
            settle(i, even)
            issue((i + 2) % PAIR, even)
            settle(i + 1, odd)
            return carry

        issue(0, even)
        if middle is None:
            lax.fori_loop(0, PAIR // 2, step, 0)
        else:
            lax.fori_loop(0, MIDDLE // 2, step, 0)
            middle()
            lax.fori_loop(MIDDLE // 2, PAIR // 2, step, 0)

        def total(p):
            value = acc[rows(p), :] + chain[links[1, p]]
            return jnp.concatenate([value[:, :HD] * SCALE, value[:, HD:]], axis=1)

        def edge_total(p, carry):
            left_grads[h, rows(p), :] = total(p).astype(BF16)
            right_grads[h, rows(p), :] = total(EDGE + PAIR + p).astype(BF16)
            return carry

        def own_total(p, carry):
            own_grads[h, rows(p), :] = total(EDGE + p)
            return carry

        lax.fori_loop(0, EDGE, edge_total, 0)
        start(back_edge_copies(h, 0))
        start(back_edge_copies(h, 1))
        lax.fori_loop(0, PAIR, own_total, 0)

    back_sends, back_locals = [], []
    parts = [slice(t * HD, (t + 1) * HD) for t in range(3)]

    def column(device, h, t):
        return out.at[:, pl.ds(pl.multiple_of((device * heads + h) * wide + t * HD, HD), HD)]

    def give(h, t):
        for k in range(1, ways):
            peer = (me + k) % ways
            copy = remote(
                joined.at[h, rows(peer), parts[t]], column(me, h, t), back_send.at[h, k, t], back_recv.at[h, k, t],
                peer_id(peer, sizes),
            )
            copy.start()
            back_sends.append(copy)
        copy = pltpu.make_async_copy(joined.at[h, rows(me), parts[t]], column(me, h, t), back_local.at[h, t])
        copy.start()
        back_locals.append(copy)

    def combine(h, part):
        arrive(back_edge_copies(h, part))
        columns = parts[part]
        for t in range(PAIR):
            value = own_grads[h, rows(t), columns]
            if t < TILES:
                near, far, table, base = from_prev, from_next, 0, t
                near_at, far_at = t, 0
            else:
                near, far, table, base = from_next, from_prev, 1, t - TILES
                near_at, far_at = NAMED + t - TILES, TILES
            value += near[h, rows(near_at), columns].astype(F32)
            for s in range(NAMED):
                term = far[h, rows(far_at + s), columns].astype(F32)
                value += jnp.where(slots[table, s] == base, term, 0.0)
            joined[h, rows(t), parts[part + 1]] = value.astype(BF16)
        give(h, part + 1)

    edges(0)
    edges(1)
    attend(0, functools.partial(edges, 2))
    give(0, 0)
    attend(1, functools.partial(edges, 3))
    give(1, 0)
    combine(0, 0)
    combine(0, 1)
    attend(2)
    give(2, 0)
    attend(3)
    give(3, 0)
    combine(1, 0)
    combine(1, 1)
    combine(2, 0)
    combine(2, 1)
    combine(3, 0)
    combine(3, 1)

    for h in range(heads):
        for t in range(3):
            for k in range(1, ways):
                source = (me + ways - k) % ways
                remote(
                    joined.at[h, rows(source), parts[t]], column(source, h, t), back_send.at[h, k, t],
                    back_recv.at[h, k, t], peer_id(source, sizes),
                ).wait_recv()
        leave(edge_copies(h))
        leave(back_edge_copies(h, 0))
        leave(back_edge_copies(h, 1))
    for copy in back_locals:
        copy.wait()
    for copy in sends + back_sends:
        copy.wait_send()
    list_other.wait_send()
    pl.when(beyond)(lambda: [c.wait_send() for c in list_side] and None)


def shards(qkv, grad_out, key_lists, live_counts):
    heads_total = lax.axis_size("head")
    ways = lax.axis_size("cx") * heads_total
    sizes = (lax.axis_size("cz"), heads_total, ways)
    heads = qkv.shape[1] // (3 * HD) // ways
    full = qkv.shape[0] * ways
    smem = pl.BlockSpec(memory_space=pltpu.SMEM)
    hbm = pl.BlockSpec(memory_space=pltpu.HBM)
    dma = pltpu.SemaphoreType.DMA
    edge = pltpu.VMEM((heads, EDGE * BLK, 2 * HD), BF16)
    return pl.pallas_call(
        functools.partial(layer_kernel, sizes),
        in_specs=[smem, smem, hbm, hbm],
        out_specs=pl.BlockSpec(memory_space=pltpu.VMEM),
        out_shape=pltpu.VMEM(qkv.shape, BF16),
        scratch_shapes=[
            pltpu.VMEM((heads, full, 4 * HD), BF16), edge, edge,
            pltpu.VMEM((heads, 2, NAMED * BLK, 2 * HD), BF16),
            pltpu.VMEM((ALL, BLK, 2 * HD), BF16),
            pltpu.VMEM((ALL * BLK, 2 * HD), F32),
            pltpu.VMEM((PAIR * LISTED + 1, BLK, 2 * HD), F32),
            pltpu.VMEM((WIDTH * BLK, 2 * HD), F32), pltpu.VMEM((WIDTH * BLK, 2 * HD), F32),
            pltpu.VMEM((heads, full, 2 * HD), F32),
            edge, edge, edge, edge,
            pltpu.VMEM((heads, full, 3 * HD), BF16),
            pltpu.VMEM((4, 8, 128), I32), pltpu.VMEM((8, 128), I32),
            pltpu.SMEM((4, 8, 128), I32), pltpu.SMEM((8, 128), I32),
            pltpu.SMEM((PAIR, LISTED), I32), pltpu.SMEM((2, NAMED), I32),
            dma((heads, ways, 3)), dma((heads, ways, 3)), dma((heads, 3)),
            dma((heads, 2, 2)), dma((heads, 2, 2)), dma((heads, 2, 2)), dma((heads, 2, 2)),
            dma((heads, ways, 3)), dma((heads, ways, 3)), dma((heads, 3)),
            dma((3,)), dma((3,)), dma((2,)),
        ],
        compiler_params=pltpu.CompilerParams(
            collective_id=0, has_side_effects=True, vmem_limit_bytes=60_000_000
        ),
        name="layer",
    )(key_lists, live_counts, qkv, grad_out)


def solution(mesh):
    ctx, head = mesh.shape["ctx"], mesh.shape["head"]
    split = Mesh(mesh.devices.reshape(ctx // 2, 2, head), ("cz", "cx", "head"))
    both = ("cz", "cx")
    tokens = P((*both, "head"), None)
    return jax.shard_map(
        shards, mesh=split, in_specs=(tokens, tokens, P(both, None), P(both)), out_specs=tokens, check_vma=False
    )
```

```python
import functools

import jax
import jax.numpy as jnp
from jax import lax
from jax.experimental import pallas as pl
from jax.experimental.pallas import tpu as pltpu
from jax.sharding import Mesh, PartitionSpec as P

HD = 128
BLK = 128
TILES = 4
LISTED = 4
NAMED = 2
PAIR = 2 * TILES
EDGE = NAMED + TILES
ALL = 2 * EDGE + PAIR
WIDTH = 3 + LISTED
SCALE = HD ** (-0.5)
RATE = SCALE * 1.4426950408889634
MESH = pl.DeviceIdType.MESH
I32 = jnp.int32
F32 = jnp.float32
BF16 = jnp.bfloat16


def rows(block, count=1):
    start = block * BLK
    return pl.ds(start if isinstance(start, int) else pl.multiple_of(start, BLK), count * BLK)


def position(sizes):
    pairs_total, heads_total, ways = sizes
    z = lax.axis_index("cz")
    me = lax.axis_index("cx") * heads_total + lax.axis_index("head")
    return z, me


def peer_id(peer, sizes):
    return {"cx": peer // sizes[1], "head": peer % sizes[1]}


def greet(sizes):
    pairs_total, _, ways = sizes
    z, me = position(sizes)
    x = lax.axis_index("cx")
    side = z - 1 + 2 * x
    inside = (side >= 0) & (side < pairs_total)
    barrier = pltpu.get_barrier_semaphore()

    def signal(device_id):
        pl.semaphore_signal(barrier, inc=1, device_id=device_id, device_id_type=MESH)

    for k in range(1, ways):
        signal(peer_id((me + k) % ways, sizes))
    pl.when(z > 0)(lambda: signal({"cz": z - 1}))
    pl.when(z < pairs_total - 1)(lambda: signal({"cz": z + 1}))
    pl.when(inside)(lambda: signal({"cz": side, "cx": 1 - x}))
    neighbours = jnp.minimum(z, 1) + jnp.minimum(pairs_total - 1 - z, 1) + jnp.where(inside, 1, 0)
    pl.semaphore_wait(barrier, ways - 1 + neighbours)


def remote(src, dst, send, recv, device_id):
    return pltpu.make_async_remote_copy(
        src_ref=src, dst_ref=dst, send_sem=send, recv_sem=recv, device_id=device_id, device_id_type=MESH
    )


def pack(lists, key_lists, live_counts, pairs_total, z, x):
    row = lax.broadcasted_iota(I32, (8, 128), 0)
    col = lax.broadcasted_iota(I32, (8, 128), 1)
    value = jnp.full((8, 128), -1, I32)
    for b in range(TILES):
        for j in range(LISTED):
            value = jnp.where((row == b) & (col == j), key_lists[b, j], value)
        value = jnp.where((row == b) & (col == LISTED), live_counts[b], value)
    lists[x] = value

    @pl.when(z == pairs_total - 1)
    def _():
        lists[2] = jnp.full((8, 128), -1, I32)

    @pl.when(z == 0)
    def _():
        lists[3] = jnp.full((8, 128), -1, I32)


def tables(tab, places, slots, chains, z):
    base = z * PAIR

    def named(run, first):
        flags = [jnp.int32(0)] * TILES
        for b in range(TILES):
            for j in range(LISTED):
                at = tab[run, b, j] - first
                flags = [jnp.where(at == t, 1, flag) for t, flag in enumerate(flags)]
        ranks = [jnp.int32(0)]
        for flag in flags[:-1]:
            ranks.append(ranks[-1] + flag)
        return flags, ranks

    for side, (run, first) in enumerate(((2, base), (3, base + TILES))):
        flags, ranks = named(run, first)
        for s in range(NAMED):
            chosen = jnp.int32(0)
            for t in range(TILES):
                chosen = jnp.where((flags[t] == 1) & (ranks[t] == s), t, chosen)
            slots[side, s] = chosen
    row = lax.broadcasted_iota(I32, (8, 128), 0)
    col = lax.broadcasted_iota(I32, (8, 128), 1)
    before = jnp.zeros((8, 128), I32)
    last = jnp.zeros((8, 128), I32)
    along = jnp.full((8, 128), -1, I32)
    found = []
    for run, (first, start) in enumerate(((base - PAIR, 0), (base + PAIR + TILES, EDGE + PAIR + TILES))):
        _, ranks = named(run, first)
        for b in range(TILES):
            for j in range(LISTED):
                block = tab[run, b, j]
                far = jnp.int32(0)
                for t in range(1, TILES):
                    far = jnp.where(block - first == t, ranks[t], far)
                outside = (block < base - TILES) if run == 0 else (block >= base + PAIR + TILES)
                place = jnp.where(outside, start + far, EDGE + block - base)
                place = jnp.clip(place, 0, ALL - 1)
                places[run * TILES + b, j] = place
                found.append(place)
    for n, place in enumerate(found):
        along = jnp.where(col == n, place, along)
    for n, place in enumerate(found):
        before = jnp.where((along == place) & (col > n), n + 1, before)
        last = jnp.where(col == place, n + 1, last)
    chains[...] = jnp.where(row == 0, before, last)


def layer_kernel(
    sizes, key_lists, live_counts, qkv, grads, out,
    own, left, right, stage, pairs, acc, chain, even, odd, own_grads, left_grads, right_grads, from_next, from_prev, joined,
    lists, chains, tab, links, places, slots,
    send, recv, edge_send, edge_recv, back_edge_send, back_edge_recv, back_send, back_recv,
    list_send, list_recv, table_sem,
):
    pairs_total, _, ways = sizes
    heads = own.shape[0]
    z, me = position(sizes)
    x = lax.axis_index("cx")
    wide, slim = 3 * HD, HD
    inner = (z > 0, z < pairs_total - 1)
    kv = pl.ds(HD, 2 * HD)
    pack(lists, key_lists, live_counts, pairs_total, z, x)
    greet(sizes)

    def piece(h, device, block, t):
        at = device * heads + h
        if t == 3:
            return grads.at[:, pl.ds(pl.multiple_of(at * slim, HD), slim)], own.at[h, rows(block), pl.ds(wide, slim)]
        column = (t + 1) % 3 * HD
        start = pl.multiple_of(at * wide + column, HD)
        return qkv.at[:, pl.ds(start, HD)], own.at[h, rows(block), pl.ds(column, HD)]

    side = z - 1 + 2 * x
    beyond = (side >= 0) & (side < pairs_total)
    list_other = remote(lists.at[x], lists.at[x], list_send.at[0], list_recv.at[0], {"cx": 1 - x})
    list_side = [
        remote(lists.at[x], lists.at[2 + x], list_send.at[1], list_recv.at[1 + x], {"cz": side}),
        remote(lists.at[x], lists.at[2 + x], list_send.at[2], list_recv.at[1 + x], {"cz": side, "cx": 1 - x}),
    ]
    list_other.start()
    pl.when(beyond)(lambda: [c.start() for c in list_side] and None)

    def fetch(h, kinds):
        for t in kinds:
            for k in range(1, ways):
                peer = (me + k) % ways
                src, dst = piece(h, peer, me, t)
                remote(src, dst, send.at[h], recv.at[h, t], peer_id(peer, sizes)).start()
            src, dst = piece(h, me, me, t)
            pltpu.make_async_copy(src, dst, recv.at[h, t]).start()

    def settled(ref, sem):
        pltpu.make_async_copy(ref, ref, sem).wait()

    def arrived(h, kinds):
        for t in kinds:
            column = 3 * HD if t == 3 else (t + 1) % 3 * HD
            settled(own.at[h, :, pl.ds(column, HD)], recv.at[h, t])

    fetch(0, (0,))
    fetch(0, (1,))
    fetch(1, (0,))
    fetch(1, (1,))
    fetch(0, (2, 3))
    fetch(2, (0,))
    fetch(2, (1,))
    fetch(1, (2, 3))
    fetch(3, (0,))
    fetch(3, (1,))
    fetch(2, (2, 3))
    fetch(3, (2, 3))

    @pl.when(z == 0)
    def _():
        left[...] = jnp.zeros_like(left)
        from_prev[...] = jnp.zeros_like(from_prev)

    @pl.when(z == pairs_total - 1)
    def _():
        right[...] = jnp.zeros_like(right)
        from_next[...] = jnp.zeros_like(from_next)

    chain[0] = jnp.zeros((BLK, 2 * HD), F32)

    list_other_in = remote(lists.at[1 - x], lists.at[1 - x], list_send.at[0], list_recv.at[0], {"cx": 1 - x})
    list_other_in.wait_recv()
    for n, there in ((0, inner[1]), (1, inner[0])):
        come = remote(lists.at[2 + n], lists.at[2 + n], list_send.at[1], list_recv.at[1 + n], {"cx": 1 - x})
        pl.when(there)(come.wait_recv)
    copy = pltpu.make_async_copy(lists, tab, table_sem.at[0])
    copy.start()
    copy.wait()
    tables(tab, places, slots, chains, z)
    copy = pltpu.make_async_copy(chains, links, table_sem.at[1])
    copy.start()
    copy.wait()

    def edge_copies(h, t):
        part = pl.ds(t * HD, HD)
        column = pl.ds((t + 1) * HD, HD)
        up = [
            remote(src, left.at[h, place, part], edge_send.at[h, 0], edge_recv.at[h, 0, t], {"cz": z + 1})
            for n, (src, place) in enumerate(
                ((stage.at[h, 0, :, part], rows(0, NAMED)), (own.at[h, rows(TILES, TILES), column], rows(NAMED, TILES)))
            )
        ]
        down = [
            remote(src, right.at[h, place, part], edge_send.at[h, 1], edge_recv.at[h, 1, t], {"cz": z - 1})
            for n, (src, place) in enumerate(
                ((stage.at[h, 1, :, part], rows(TILES, NAMED)), (own.at[h, rows(0, TILES), column], rows(0, TILES)))
            )
        ]
        return up, down

    def back_edge_copies(h, t):
        part = pl.ds(t * HD, HD)
        up = remote(
            right_grads.at[h, :, part], from_prev.at[h, :, part],
            back_edge_send.at[h, 0], back_edge_recv.at[h, 0, t], {"cz": z + 1},
        )
        down = remote(
            left_grads.at[h, :, part], from_next.at[h, :, part],
            back_edge_send.at[h, 1], back_edge_recv.at[h, 1, t], {"cz": z - 1},
        )
        return [up], [down]

    def start(copies):
        up, down = copies
        pl.when(inner[1])(lambda: [c.start() for c in up] and None)
        pl.when(inner[0])(lambda: [c.start() for c in down] and None)

    def arrive(h, t, refs, sems):
        part = pl.ds(t * HD, HD)
        pl.when(inner[0])(lambda: settled(refs[0].at[h, :, part], sems.at[h, 0, t]))
        pl.when(inner[1])(lambda: settled(refs[1].at[h, :, part], sems.at[h, 1, t]))

    def leave(h, refs, sems):
        pl.when(inner[1])(lambda: settled(refs[0].at[h], sems.at[h, 0]))
        pl.when(inner[0])(lambda: settled(refs[1].at[h], sems.at[h, 1]))

    def edges(h, t):
        arrived(h, (t,))
        columns = slice((t + 1) * HD, (t + 2) * HD)
        for s in range(NAMED):
            for side in range(2):
                chosen = own[h, rows(side * TILES), columns]
                for n in range(1, TILES):
                    chosen = jnp.where(slots[side, s] == n, own[h, rows(side * TILES + n), columns], chosen)
                stage[h, side, rows(s), t * HD : (t + 1) * HD] = chosen
        start(edge_copies(h, t))

    def attend(h, plan=()):
        arrived(h, (2, 3))
        arrive(h, 0, (left, right), edge_recv)
        arrive(h, 1, (left, right), edge_recv)
        pairs[:EDGE] = left[h].reshape(EDGE, BLK, 2 * HD)
        pairs[EDGE : EDGE + PAIR] = own[h, :, HD : 3 * HD].reshape(PAIR, BLK, 2 * HD)
        pairs[EDGE + PAIR :] = right[h].reshape(EDGE, BLK, 2 * HD)
        acc[...] = jnp.zeros_like(acc)

        def operand(i):
            q = own[h, rows(i), :HD]
            g = own[h, rows(i), 3 * HD :]
            zero = jnp.zeros_like(q)
            return jnp.concatenate(
                [jnp.concatenate([q, zero], axis=1), jnp.concatenate([zero, g], axis=1)], axis=0
            )

        def keys(i, columns):
            near = [pairs[EDGE - 1 + i + n, :, columns] for n in range(3)]
            return jnp.concatenate(near + [pairs[places[i, j], :, columns] for j in range(LISTED)], axis=0)

        def issue(i, slot):
            slot[...] = lax.dot_general(
                keys(i, slice(None)), operand(i), (((1,), (1,)), ((), ())), preferred_element_type=F32
            )

        def settle(i, products):
            block = z * PAIR + i
            live = tab[i // TILES, i % TILES, LISTED]
            usable = [block > 0, None, block < pairs_total * PAIR - 1] + [live > j for j in range(LISTED)]
            tiles = [products[n * BLK : (n + 1) * BLK, :HD] for n in range(WIDTH)]
            peaks = [jnp.max(s.reshape(BLK // 8, 8, HD), axis=0) for s in tiles]
            peaks = [s if ok is None else jnp.where(ok, s, -1e30) for s, ok in zip(peaks, usable)]
            shift = jnp.max(functools.reduce(jnp.maximum, peaks), axis=0, keepdims=True) * -RATE
            shifts = [shift if ok is None else jnp.where(ok, shift, -1e30) for ok in usable]
            powers = jnp.concatenate([jnp.exp2(s * RATE + b) for s, b in zip(tiles, shifts)], axis=0)
            dp = products[:, HD:]
            over = 1.0 / jnp.sum(powers, axis=0, keepdims=True)
            soft = powers * over
            ds = soft * (dp - jnp.sum(powers * dp, axis=0, keepdims=True) * over)
            ds_low = ds.astype(BF16)
            low = jnp.concatenate([ds_low, soft.astype(BF16)], axis=1)
            terms = jnp.dot(low, operand(i), preferred_element_type=F32)
            grad_q = lax.dot_general(
                ds_low, keys(i, slice(0, HD)), (((0,), (0,)), ((), ())), preferred_element_type=F32
            )
            joined[h, rows(i), :HD] = (grad_q * SCALE).astype(BF16)
            acc[rows(EDGE - 1 + i, 3), :] += terms[: 3 * BLK]
            for j in range(LISTED):
                n = i * LISTED + j
                chain[n + 1] = terms[(3 + j) * BLK : (4 + j) * BLK] + chain[links[0, n]]

        def step(n, carry):
            i = 2 * n
            for when, task in plan:
                pl.when(n == when)(task)
            issue(i + 1, odd)
            settle(i, even)
            issue((i + 2) % PAIR, even)
            settle(i + 1, odd)
            return carry

        issue(0, even)
        lax.fori_loop(0, PAIR // 2, step, 0)

        def total(p):
            value = acc[rows(p), :] + chain[links[1, p]]
            return jnp.concatenate([value[:, :HD] * SCALE, value[:, HD:]], axis=1)

        def edge_total(p, carry):
            left_grads[h, rows(p), :] = total(p).astype(BF16)
            right_grads[h, rows(p), :] = total(EDGE + PAIR + p).astype(BF16)
            return carry

        def own_total(p, carry):
            own_grads[h, rows(p), :] = total(EDGE + p)
            return carry

        lax.fori_loop(0, EDGE, edge_total, 0)
        start(back_edge_copies(h, 0))
        start(back_edge_copies(h, 1))
        lax.fori_loop(0, PAIR, own_total, 0)

    parts = [slice(t * HD, (t + 1) * HD) for t in range(3)]

    def column(device, h, t):
        return out.at[:, pl.ds(pl.multiple_of((device * heads + h) * wide + t * HD, HD), HD)]

    def give_copy(h, t, k):
        peer = (me + k) % ways
        return remote(
            joined.at[h, rows(peer), parts[t]], column(me, h, t), back_send.at[h], back_recv.at[h],
            peer_id(peer, sizes),
        )

    def give_local(h, t):
        return pltpu.make_async_copy(joined.at[h, rows(me), parts[t]], column(me, h, t), back_recv.at[h])

    def give(h, t):
        for k in range(1, ways):
            give_copy(h, t, k).start()
        give_local(h, t).start()

    def combine(h, part):
        arrive(h, part, (from_prev, from_next), back_edge_recv)
        columns = parts[part]
        for t in range(PAIR):
            value = own_grads[h, rows(t), columns]
            if t < TILES:
                near, far, table, base = from_prev, from_next, 0, t
                near_at, far_at = t, 0
            else:
                near, far, table, base = from_next, from_prev, 1, t - TILES
                near_at, far_at = NAMED + t - TILES, TILES
            value += near[h, rows(near_at), columns].astype(F32)
            for s in range(NAMED):
                term = far[h, rows(far_at + s), columns].astype(F32)
                value += jnp.where(slots[table, s] == base, term, 0.0)
            joined[h, rows(t), parts[part + 1]] = value.astype(BF16)
        give(h, part + 1)

    edges(0, 0)
    edges(0, 1)
    edges(1, 0)
    edges(1, 1)
    attend(0, [(2, functools.partial(edges, 2, 0)), (2, functools.partial(edges, 2, 1))])
    give(0, 0)
    attend(1, [(2, functools.partial(edges, 3, 0)), (2, functools.partial(edges, 3, 1))])
    give(1, 0)
    combine(0, 0)
    combine(0, 1)
    attend(2)
    give(2, 0)
    attend(3)
    give(3, 0)
    combine(1, 0)
    combine(1, 1)
    combine(2, 0)
    combine(2, 1)
    combine(3, 0)
    combine(3, 1)

    for h in range(heads):
        settled(own.at[h, pl.ds(0, (ways - 1) * BLK)], send.at[h])
        leave(h, (left, right), edge_send)
        leave(h, (right_grads, left_grads), back_edge_send)
        settled(joined.at[h, pl.ds(0, (ways - 1) * BLK)], back_send.at[h])
        settled(out.at[:, pl.ds(0, ways * wide)], back_recv.at[h])
    list_other.wait_send()
    pl.when(beyond)(lambda: [c.wait_send() for c in list_side] and None)


def shards(qkv, grad_out, key_lists, live_counts):
    heads_total = lax.axis_size("head")
    ways = lax.axis_size("cx") * heads_total
    sizes = (lax.axis_size("cz"), heads_total, ways)
    heads = qkv.shape[1] // (3 * HD) // ways
    full = qkv.shape[0] * ways
    smem = pl.BlockSpec(memory_space=pltpu.SMEM)
    hbm = pl.BlockSpec(memory_space=pltpu.HBM)
    dma = pltpu.SemaphoreType.DMA
    edge = pltpu.VMEM((heads, EDGE * BLK, 2 * HD), BF16)
    return pl.pallas_call(
        functools.partial(layer_kernel, sizes),
        in_specs=[smem, smem, hbm, hbm],
        out_specs=pl.BlockSpec(memory_space=pltpu.VMEM),
        out_shape=pltpu.VMEM(qkv.shape, BF16),
        scratch_shapes=[
            pltpu.VMEM((heads, full, 4 * HD), BF16), edge, edge,
            pltpu.VMEM((heads, 2, NAMED * BLK, 2 * HD), BF16),
            pltpu.VMEM((ALL, BLK, 2 * HD), BF16),
            pltpu.VMEM((ALL * BLK, 2 * HD), F32),
            pltpu.VMEM((PAIR * LISTED + 1, BLK, 2 * HD), F32),
            pltpu.VMEM((WIDTH * BLK, 2 * HD), F32), pltpu.VMEM((WIDTH * BLK, 2 * HD), F32),
            pltpu.VMEM((heads, full, 2 * HD), F32),
            edge, edge, edge, edge,
            pltpu.VMEM((heads, full, 3 * HD), BF16),
            pltpu.VMEM((4, 8, 128), I32), pltpu.VMEM((8, 128), I32),
            pltpu.SMEM((4, 8, 128), I32), pltpu.SMEM((8, 128), I32),
            pltpu.SMEM((PAIR, LISTED), I32), pltpu.SMEM((2, NAMED), I32),
            dma((heads,)), dma((heads, 4)),
            dma((heads, 2)), dma((heads, 2, 2)), dma((heads, 2)), dma((heads, 2, 2)),
            dma((heads,)), dma((heads,)),
            dma((3,)), dma((3,)), dma((2,)),
        ],
        compiler_params=pltpu.CompilerParams(
            collective_id=0, has_side_effects=True, vmem_limit_bytes=60_000_000
        ),
        name="layer",
    )(key_lists, live_counts, qkv, grad_out)


def solution(mesh):
    ctx, head = mesh.shape["ctx"], mesh.shape["head"]
    split = Mesh(mesh.devices.reshape(ctx // 2, 2, head), ("cz", "cx", "head"))
    both = ("cz", "cx")
    tokens = P((*both, "head"), None)
    return jax.shard_map(
        shards, mesh=split, in_specs=(tokens, tokens, P(both, None), P(both)), out_specs=tokens, check_vma=False
    )
```

```python
import functools

import jax
import jax.numpy as jnp
from jax import lax
from jax.experimental import pallas as pl
from jax.experimental.pallas import tpu as pltpu
from jax.sharding import Mesh, PartitionSpec as P

HD = 128
BLK = 128
TILES = 4
LISTED = 4
NAMED = 2
PAIR = 2 * TILES
EDGE = NAMED + TILES
ALL = 2 * EDGE + PAIR
WIDTH = 3 + LISTED
SCALE = HD ** (-0.5)
RATE = SCALE * 1.4426950408889634
MESH = pl.DeviceIdType.MESH
I32 = jnp.int32
F32 = jnp.float32
BF16 = jnp.bfloat16


def rows(block, count=1):
    start = block * BLK
    return pl.ds(start if isinstance(start, int) else pl.multiple_of(start, BLK), count * BLK)


def position(sizes):
    pairs_total, heads_total, ways = sizes
    z = lax.axis_index("cz")
    me = lax.axis_index("cx") * heads_total + lax.axis_index("head")
    return z, me


def peer_id(peer, sizes):
    return {"cx": peer // sizes[1], "head": peer % sizes[1]}


def greet(sizes):
    pairs_total, _, ways = sizes
    z, me = position(sizes)
    x = lax.axis_index("cx")
    side = z - 1 + 2 * x
    inside = (side >= 0) & (side < pairs_total)
    barrier = pltpu.get_barrier_semaphore()

    def signal(device_id):
        pl.semaphore_signal(barrier, inc=1, device_id=device_id, device_id_type=MESH)

    for k in range(1, ways):
        signal(peer_id((me + k) % ways, sizes))
    pl.when(z > 0)(lambda: signal({"cz": z - 1}))
    pl.when(z < pairs_total - 1)(lambda: signal({"cz": z + 1}))
    pl.when(inside)(lambda: signal({"cz": side, "cx": 1 - x}))
    neighbours = jnp.minimum(z, 1) + jnp.minimum(pairs_total - 1 - z, 1) + jnp.where(inside, 1, 0)
    pl.semaphore_wait(barrier, ways - 1 + neighbours)


def remote(src, dst, send, recv, device_id):
    return pltpu.make_async_remote_copy(
        src_ref=src, dst_ref=dst, send_sem=send, recv_sem=recv, device_id=device_id, device_id_type=MESH
    )


def pack(lists, key_lists, live_counts, pairs_total, z, x):
    row = lax.broadcasted_iota(I32, (8, 128), 0)
    col = lax.broadcasted_iota(I32, (8, 128), 1)
    value = jnp.full((8, 128), -1, I32)
    for b in range(TILES):
        for j in range(LISTED):
            value = jnp.where((row == b) & (col == j), key_lists[b, j], value)
        value = jnp.where((row == b) & (col == LISTED), live_counts[b], value)
    lists[x] = value

    @pl.when(z == pairs_total - 1)
    def _():
        lists[2] = jnp.full((8, 128), -1, I32)

    @pl.when(z == 0)
    def _():
        lists[3] = jnp.full((8, 128), -1, I32)


def tables(tab, places, slots, chains, z):
    base = z * PAIR

    def named(run, first):
        flags = [jnp.int32(0)] * TILES
        for b in range(TILES):
            for j in range(LISTED):
                at = tab[run, b, j] - first
                flags = [jnp.where(at == t, 1, flag) for t, flag in enumerate(flags)]
        ranks = [jnp.int32(0)]
        for flag in flags[:-1]:
            ranks.append(ranks[-1] + flag)
        return flags, ranks

    for side, (run, first) in enumerate(((2, base), (3, base + TILES))):
        flags, ranks = named(run, first)
        for s in range(NAMED):
            chosen = jnp.int32(0)
            for t in range(TILES):
                chosen = jnp.where((flags[t] == 1) & (ranks[t] == s), t, chosen)
            slots[side, s] = chosen
    row = lax.broadcasted_iota(I32, (8, 128), 0)
    col = lax.broadcasted_iota(I32, (8, 128), 1)
    before = jnp.zeros((8, 128), I32)
    last = jnp.zeros((8, 128), I32)
    along = jnp.full((8, 128), -1, I32)
    found = []
    for run, (first, start) in enumerate(((base - PAIR, 0), (base + PAIR + TILES, EDGE + PAIR + TILES))):
        _, ranks = named(run, first)
        for b in range(TILES):
            for j in range(LISTED):
                block = tab[run, b, j]
                far = jnp.int32(0)
                for t in range(1, TILES):
                    far = jnp.where(block - first == t, ranks[t], far)
                outside = (block < base - TILES) if run == 0 else (block >= base + PAIR + TILES)
                place = jnp.where(outside, start + far, EDGE + block - base)
                place = jnp.clip(place, 0, ALL - 1)
                places[run * TILES + b, j] = place
                found.append(place)
    for n, place in enumerate(found):
        along = jnp.where(col == n, place, along)
    for n, place in enumerate(found):
        before = jnp.where((along == place) & (col > n), n + 1, before)
        last = jnp.where(col == place, n + 1, last)
    chains[...] = jnp.where(row == 0, before, last)


def layer_kernel(
    sizes, key_lists, live_counts, qkv, grads, out,
    own, left, right, stage, pairs, acc, chain, even, odd, own_grads, left_grads, right_grads, from_next, from_prev, joined,
    lists, chains, tab, links, places, slots, named_here, live_here,
    send, recv, edge_send, edge_recv, back_edge_send, back_edge_recv, back_send, back_recv,
    list_send, list_recv, table_sem,
):
    pairs_total, _, ways = sizes
    heads = own.shape[0]
    z, me = position(sizes)
    x = lax.axis_index("cx")
    wide, slim = 3 * HD, HD
    inner = (z > 0, z < pairs_total - 1)
    kv = pl.ds(HD, 2 * HD)
    own_lists = pltpu.make_async_copy(key_lists, named_here, table_sem.at[0])
    own_counts = pltpu.make_async_copy(live_counts, live_here, table_sem.at[1])
    own_lists.start()
    own_counts.start()
    greet(sizes)

    def piece(h, device, block, t):
        at = device * heads + h
        if t == 3:
            return grads.at[:, pl.ds(pl.multiple_of(at * slim, HD), slim)], own.at[h, rows(block), pl.ds(wide, slim)]
        column = (t + 1) % 3 * HD
        start = pl.multiple_of(at * wide + column, HD)
        return qkv.at[:, pl.ds(start, HD)], own.at[h, rows(block), pl.ds(column, HD)]

    side = z - 1 + 2 * x
    beyond = (side >= 0) & (side < pairs_total)
    list_other = remote(lists.at[x], lists.at[x], list_send.at[0], list_recv.at[0], {"cx": 1 - x})
    list_side = [
        remote(lists.at[x], lists.at[2 + x], list_send.at[1], list_recv.at[1 + x], {"cz": side}),
        remote(lists.at[x], lists.at[2 + x], list_send.at[2], list_recv.at[1 + x], {"cz": side, "cx": 1 - x}),
    ]
    def fetch(h, kinds):
        for t in kinds:
            for k in range(1, ways):
                peer = (me + k) % ways
                src, dst = piece(h, peer, me, t)
                remote(src, dst, send.at[h], recv.at[h, t], peer_id(peer, sizes)).start()
            src, dst = piece(h, me, me, t)
            pltpu.make_async_copy(src, dst, recv.at[h, t]).start()

    own_lists.wait()
    own_counts.wait()
    pack(lists, named_here, live_here, pairs_total, z, x)
    list_other.start()
    pl.when(beyond)(lambda: [c.start() for c in list_side] and None)

    def settled(ref, sem):
        pltpu.make_async_copy(ref, ref, sem).wait()

    def arrived(h, kinds):
        for t in kinds:
            column = 3 * HD if t == 3 else (t + 1) % 3 * HD
            settled(own.at[h, :, pl.ds(column, HD)], recv.at[h, t])

    fetch(0, (0,))
    fetch(0, (1,))

    fetch(1, (0,))
    fetch(1, (1,))
    fetch(0, (2, 3))
    fetch(2, (0,))
    fetch(2, (1,))
    fetch(1, (2, 3))
    fetch(3, (0,))
    fetch(3, (1,))
    fetch(2, (2, 3))
    fetch(3, (2, 3))

    @pl.when(z == 0)
    def _():
        left[...] = jnp.zeros_like(left)
        from_prev[...] = jnp.zeros_like(from_prev)

    @pl.when(z == pairs_total - 1)
    def _():
        right[...] = jnp.zeros_like(right)
        from_next[...] = jnp.zeros_like(from_next)

    chain[0] = jnp.zeros((BLK, 2 * HD), F32)

    list_other_in = remote(lists.at[1 - x], lists.at[1 - x], list_send.at[0], list_recv.at[0], {"cx": 1 - x})
    list_other_in.wait_recv()
    for n, there in ((0, inner[1]), (1, inner[0])):
        come = remote(lists.at[2 + n], lists.at[2 + n], list_send.at[1], list_recv.at[1 + n], {"cx": 1 - x})
        pl.when(there)(come.wait_recv)
    copy = pltpu.make_async_copy(lists, tab, table_sem.at[0])
    copy.start()
    copy.wait()
    tables(tab, places, slots, chains, z)
    copy = pltpu.make_async_copy(chains, links, table_sem.at[1])
    copy.start()
    copy.wait()

    def edge_copies(h, t):
        part = pl.ds(t * HD, HD)
        column = pl.ds((t + 1) * HD, HD)
        up = [
            remote(src, left.at[h, place, part], edge_send.at[h, 0], edge_recv.at[h, 0, t], {"cz": z + 1})
            for n, (src, place) in enumerate(
                ((stage.at[h, 0, :, part], rows(0, NAMED)), (own.at[h, rows(TILES, TILES), column], rows(NAMED, TILES)))
            )
        ]
        down = [
            remote(src, right.at[h, place, part], edge_send.at[h, 1], edge_recv.at[h, 1, t], {"cz": z - 1})
            for n, (src, place) in enumerate(
                ((stage.at[h, 1, :, part], rows(TILES, NAMED)), (own.at[h, rows(0, TILES), column], rows(0, TILES)))
            )
        ]
        return up, down

    def back_edge_copies(h, t):
        part = pl.ds(t * HD, HD)
        up = remote(
            right_grads.at[h, :, part], from_prev.at[h, :, part],
            back_edge_send.at[h, 0], back_edge_recv.at[h, 0, t], {"cz": z + 1},
        )
        down = remote(
            left_grads.at[h, :, part], from_next.at[h, :, part],
            back_edge_send.at[h, 1], back_edge_recv.at[h, 1, t], {"cz": z - 1},
        )
        return [up], [down]

    def start(copies):
        up, down = copies
        pl.when(inner[1])(lambda: [c.start() for c in up] and None)
        pl.when(inner[0])(lambda: [c.start() for c in down] and None)

    def arrive(h, t, refs, sems):
        part = pl.ds(t * HD, HD)
        pl.when(inner[0])(lambda: settled(refs[0].at[h, :, part], sems.at[h, 0, t]))
        pl.when(inner[1])(lambda: settled(refs[1].at[h, :, part], sems.at[h, 1, t]))

    def leave(h, refs, sems):
        pl.when(inner[1])(lambda: settled(refs[0].at[h], sems.at[h, 0]))
        pl.when(inner[0])(lambda: settled(refs[1].at[h], sems.at[h, 1]))

    def edges(h, t):
        arrived(h, (t,))
        columns = slice((t + 1) * HD, (t + 2) * HD)
        for s in range(NAMED):
            for side in range(2):
                chosen = own[h, rows(side * TILES), columns]
                for n in range(1, TILES):
                    chosen = jnp.where(slots[side, s] == n, own[h, rows(side * TILES + n), columns], chosen)
                stage[h, side, rows(s), t * HD : (t + 1) * HD] = chosen
        start(edge_copies(h, t))

    def attend(h, plan=()):
        arrived(h, (2, 3))
        arrive(h, 0, (left, right), edge_recv)
        arrive(h, 1, (left, right), edge_recv)
        pairs[:EDGE] = left[h].reshape(EDGE, BLK, 2 * HD)
        pairs[EDGE : EDGE + PAIR] = own[h, :, HD : 3 * HD].reshape(PAIR, BLK, 2 * HD)
        pairs[EDGE + PAIR :] = right[h].reshape(EDGE, BLK, 2 * HD)
        acc[...] = jnp.zeros_like(acc)

        def operand(i):
            q = own[h, rows(i), :HD]
            g = own[h, rows(i), 3 * HD :]
            zero = jnp.zeros_like(q)
            return jnp.concatenate(
                [jnp.concatenate([q, zero], axis=1), jnp.concatenate([zero, g], axis=1)], axis=0
            )

        def keys(i, columns):
            near = [pairs[EDGE - 1 + i + n, :, columns] for n in range(3)]
            return jnp.concatenate(near + [pairs[places[i, j], :, columns] for j in range(LISTED)], axis=0)

        def issue(i, slot):
            slot[...] = lax.dot_general(
                keys(i, slice(None)), operand(i), (((1,), (1,)), ((), ())), preferred_element_type=F32
            )

        def settle(i, products):
            block = z * PAIR + i
            live = tab[i // TILES, i % TILES, LISTED]
            usable = [block > 0, None, block < pairs_total * PAIR - 1] + [live > j for j in range(LISTED)]
            tiles = [products[n * BLK : (n + 1) * BLK, :HD] for n in range(WIDTH)]
            peaks = [jnp.max(s.reshape(BLK // 8, 8, HD), axis=0) for s in tiles]
            peaks = [s if ok is None else jnp.where(ok, s, -1e30) for s, ok in zip(peaks, usable)]
            shift = jnp.max(functools.reduce(jnp.maximum, peaks), axis=0, keepdims=True) * -RATE
            shifts = [shift if ok is None else jnp.where(ok, shift, -1e30) for ok in usable]
            powers = jnp.concatenate([jnp.exp2(s * RATE + b) for s, b in zip(tiles, shifts)], axis=0)
            dp = products[:, HD:]
            over = 1.0 / jnp.sum(powers, axis=0, keepdims=True)
            soft = powers * over
            ds = soft * (dp - jnp.sum(powers * dp, axis=0, keepdims=True) * over)
            ds_low = ds.astype(BF16)
            low = jnp.concatenate([ds_low, soft.astype(BF16)], axis=1)
            terms = jnp.dot(low, operand(i), preferred_element_type=F32)
            grad_q = lax.dot_general(
                ds_low, keys(i, slice(0, HD)), (((0,), (0,)), ((), ())), preferred_element_type=F32
            )
            joined[h, rows(i), :HD] = (grad_q * SCALE).astype(BF16)
            acc[rows(EDGE - 1 + i, 3), :] += terms[: 3 * BLK]
            for j in range(LISTED):
                n = i * LISTED + j
                chain[n + 1] = terms[(3 + j) * BLK : (4 + j) * BLK] + chain[links[0, n]]

        def step(n, carry):
            i = 2 * n
            for when, task in plan:
                pl.when(n == when)(task)
            issue(i + 1, odd)
            settle(i, even)
            issue((i + 2) % PAIR, even)
            settle(i + 1, odd)
            return carry

        issue(0, even)
        lax.fori_loop(0, PAIR // 2, step, 0)

        def total(p):
            value = acc[rows(p), :] + chain[links[1, p]]
            return jnp.concatenate([value[:, :HD] * SCALE, value[:, HD:]], axis=1)

        def edge_total(p, carry):
            left_grads[h, rows(p), :] = total(p).astype(BF16)
            right_grads[h, rows(p), :] = total(EDGE + PAIR + p).astype(BF16)
            return carry

        def own_total(p, carry):
            own_grads[h, rows(p), :] = total(EDGE + p)
            return carry

        lax.fori_loop(0, EDGE, edge_total, 0)
        start(back_edge_copies(h, 0))
        start(back_edge_copies(h, 1))
        lax.fori_loop(0, PAIR, own_total, 0)

    parts = [slice(t * HD, (t + 1) * HD) for t in range(3)]

    def column(device, h, t):
        return out.at[:, pl.ds(pl.multiple_of((device * heads + h) * wide + t * HD, HD), HD)]

    def give_copy(h, t, k):
        peer = (me + k) % ways
        return remote(
            joined.at[h, rows(peer), parts[t]], column(me, h, t), back_send.at[h], back_recv.at[h],
            peer_id(peer, sizes),
        )

    def give_local(h, t):
        return pltpu.make_async_copy(joined.at[h, rows(me), parts[t]], column(me, h, t), back_recv.at[h])

    def give(h, t):
        for k in range(1, ways):
            give_copy(h, t, k).start()
        give_local(h, t).start()

    def combine(h, part):
        arrive(h, part, (from_prev, from_next), back_edge_recv)
        columns = parts[part]
        for t in range(PAIR):
            value = own_grads[h, rows(t), columns]
            if t < TILES:
                near, far, table, base = from_prev, from_next, 0, t
                near_at, far_at = t, 0
            else:
                near, far, table, base = from_next, from_prev, 1, t - TILES
                near_at, far_at = NAMED + t - TILES, TILES
            value += near[h, rows(near_at), columns].astype(F32)
            for s in range(NAMED):
                term = far[h, rows(far_at + s), columns].astype(F32)
                value += jnp.where(slots[table, s] == base, term, 0.0)
            joined[h, rows(t), parts[part + 1]] = value.astype(BF16)
        give(h, part + 1)

    edges(0, 0)
    edges(0, 1)
    edges(1, 0)
    edges(1, 1)
    attend(0, [(2, functools.partial(edges, 2, 0)), (2, functools.partial(edges, 2, 1))])
    give(0, 0)
    attend(1, [(2, functools.partial(edges, 3, 0)), (2, functools.partial(edges, 3, 1))])
    give(1, 0)
    combine(0, 0)
    combine(0, 1)
    attend(2)
    give(2, 0)
    attend(3)
    give(3, 0)
    combine(1, 0)
    combine(1, 1)
    combine(2, 0)
    combine(2, 1)
    combine(3, 0)
    combine(3, 1)

    for h in range(heads):
        settled(own.at[h, pl.ds(0, (ways - 1) * BLK)], send.at[h])
        leave(h, (left, right), edge_send)
        leave(h, (right_grads, left_grads), back_edge_send)
        settled(joined.at[h, pl.ds(0, (ways - 1) * BLK)], back_send.at[h])
        settled(out.at[:, pl.ds(0, ways * wide)], back_recv.at[h])
    list_other.wait_send()
    pl.when(beyond)(lambda: [c.wait_send() for c in list_side] and None)


def shards(qkv, grad_out, key_lists, live_counts):
    heads_total = lax.axis_size("head")
    ways = lax.axis_size("cx") * heads_total
    sizes = (lax.axis_size("cz"), heads_total, ways)
    heads = qkv.shape[1] // (3 * HD) // ways
    full = qkv.shape[0] * ways
    hbm = pl.BlockSpec(memory_space=pltpu.HBM)
    dma = pltpu.SemaphoreType.DMA
    edge = pltpu.VMEM((heads, EDGE * BLK, 2 * HD), BF16)
    return pl.pallas_call(
        functools.partial(layer_kernel, sizes),
        in_specs=[hbm] * 4,
        out_specs=pl.BlockSpec(memory_space=pltpu.VMEM),
        out_shape=pltpu.VMEM(qkv.shape, BF16),
        scratch_shapes=[
            pltpu.VMEM((heads, full, 4 * HD), BF16), edge, edge,
            pltpu.VMEM((heads, 2, NAMED * BLK, 2 * HD), BF16),
            pltpu.VMEM((ALL, BLK, 2 * HD), BF16),
            pltpu.VMEM((ALL * BLK, 2 * HD), F32),
            pltpu.VMEM((PAIR * LISTED + 1, BLK, 2 * HD), F32),
            pltpu.VMEM((WIDTH * BLK, 2 * HD), F32), pltpu.VMEM((WIDTH * BLK, 2 * HD), F32),
            pltpu.VMEM((heads, full, 2 * HD), F32),
            edge, edge, edge, edge,
            pltpu.VMEM((heads, full, 3 * HD), BF16),
            pltpu.VMEM((4, 8, 128), I32), pltpu.VMEM((8, 128), I32),
            pltpu.SMEM((4, 8, 128), I32), pltpu.SMEM((8, 128), I32),
            pltpu.SMEM((PAIR, LISTED), I32), pltpu.SMEM((2, NAMED), I32),
            pltpu.SMEM((TILES, LISTED), I32), pltpu.SMEM((TILES,), I32),
            dma((heads,)), dma((heads, 4)),
            dma((heads, 2)), dma((heads, 2, 2)), dma((heads, 2)), dma((heads, 2, 2)),
            dma((heads,)), dma((heads,)),
            dma((3,)), dma((3,)), dma((2,)),
        ],
        compiler_params=pltpu.CompilerParams(
            collective_id=0, has_side_effects=True, vmem_limit_bytes=60_000_000
        ),
        name="layer",
    )(key_lists, live_counts, qkv, grad_out)


def solution(mesh):
    ctx, head = mesh.shape["ctx"], mesh.shape["head"]
    split = Mesh(mesh.devices.reshape(ctx // 2, 2, head), ("cz", "cx", "head"))
    both = ("cz", "cx")
    tokens = P((*both, "head"), None)
    return jax.shard_map(
        shards, mesh=split, in_specs=(tokens, tokens, P(both, None), P(both)), out_specs=tokens, check_vma=False
    )
```

```python
import functools

import jax
import jax.numpy as jnp
from jax import lax
from jax.experimental import pallas as pl
from jax.experimental.pallas import tpu as pltpu
from jax.sharding import Mesh, PartitionSpec as P

HD = 128
BLK = 128
TILES = 4
LISTED = 4
NAMED = 2
PAIR = 2 * TILES
EDGE = NAMED + TILES
ALL = 2 * EDGE + PAIR
WIDTH = 3 + LISTED
SCALE = HD ** (-0.5)
RATE = SCALE * 1.4426950408889634
MESH = pl.DeviceIdType.MESH
I32 = jnp.int32
F32 = jnp.float32
BF16 = jnp.bfloat16


def rows(block, count=1):
    start = block * BLK
    return pl.ds(start if isinstance(start, int) else pl.multiple_of(start, BLK), count * BLK)


def position(sizes):
    pairs_total, heads_total, ways = sizes
    z = lax.axis_index("cz")
    me = lax.axis_index("cx") * heads_total + lax.axis_index("head")
    return z, me


def peer_id(peer, sizes):
    return {"cx": peer // sizes[1], "head": peer % sizes[1]}


def greet(sizes):
    pairs_total, _, ways = sizes
    z, me = position(sizes)
    x = lax.axis_index("cx")
    side = z - 1 + 2 * x
    inside = (side >= 0) & (side < pairs_total)
    barrier = pltpu.get_barrier_semaphore()

    def signal(device_id):
        pl.semaphore_signal(barrier, inc=1, device_id=device_id, device_id_type=MESH)

    for k in range(1, ways):
        signal(peer_id((me + k) % ways, sizes))
    pl.when(z > 0)(lambda: signal({"cz": z - 1}))
    pl.when(z < pairs_total - 1)(lambda: signal({"cz": z + 1}))
    pl.when(inside)(lambda: signal({"cz": side, "cx": 1 - x}))
    neighbours = jnp.minimum(z, 1) + jnp.minimum(pairs_total - 1 - z, 1) + jnp.where(inside, 1, 0)
    pl.semaphore_wait(barrier, ways - 1 + neighbours)


def remote(src, dst, send, recv, device_id):
    return pltpu.make_async_remote_copy(
        src_ref=src, dst_ref=dst, send_sem=send, recv_sem=recv, device_id=device_id, device_id_type=MESH
    )


def pack(lists, key_lists, live_counts, pairs_total, z, x):
    row = lax.broadcasted_iota(I32, (8, 128), 0)
    col = lax.broadcasted_iota(I32, (8, 128), 1)
    value = jnp.full((8, 128), -1, I32)
    for b in range(TILES):
        for j in range(LISTED):
            value = jnp.where((row == b) & (col == j), key_lists[b, j], value)
        value = jnp.where((row == b) & (col == LISTED), live_counts[b], value)
    lists[x] = value

    @pl.when(z == pairs_total - 1)
    def _():
        lists[2] = jnp.full((8, 128), -1, I32)

    @pl.when(z == 0)
    def _():
        lists[3] = jnp.full((8, 128), -1, I32)


def tables(tab, places, slots, chains, z):
    base = z * PAIR

    def named(run, first):
        flags = [jnp.int32(0)] * TILES
        for b in range(TILES):
            for j in range(LISTED):
                at = tab[run, b, j] - first
                flags = [jnp.where(at == t, 1, flag) for t, flag in enumerate(flags)]
        ranks = [jnp.int32(0)]
        for flag in flags[:-1]:
            ranks.append(ranks[-1] + flag)
        return flags, ranks

    for side, (run, first) in enumerate(((2, base), (3, base + TILES))):
        flags, ranks = named(run, first)
        for s in range(NAMED):
            chosen = jnp.int32(0)
            for t in range(TILES):
                chosen = jnp.where((flags[t] == 1) & (ranks[t] == s), t, chosen)
            slots[side, s] = chosen
    row = lax.broadcasted_iota(I32, (8, 128), 0)
    col = lax.broadcasted_iota(I32, (8, 128), 1)
    before = jnp.zeros((8, 128), I32)
    last = jnp.zeros((8, 128), I32)
    along = jnp.full((8, 128), -1, I32)
    found = []
    for run, (first, start) in enumerate(((base - PAIR, 0), (base + PAIR + TILES, EDGE + PAIR + TILES))):
        _, ranks = named(run, first)
        for b in range(TILES):
            for j in range(LISTED):
                block = tab[run, b, j]
                far = jnp.int32(0)
                for t in range(1, TILES):
                    far = jnp.where(block - first == t, ranks[t], far)
                outside = (block < base - TILES) if run == 0 else (block >= base + PAIR + TILES)
                place = jnp.where(outside, start + far, EDGE + block - base)
                place = jnp.clip(place, 0, ALL - 1)
                places[run * TILES + b, j] = place
                found.append(place)
    for n, place in enumerate(found):
        along = jnp.where(col == n, place, along)
    for n, place in enumerate(found):
        before = jnp.where((along == place) & (col > n), n + 1, before)
        last = jnp.where(col == place, n + 1, last)
    chains[...] = jnp.where(row == 0, before, last)


def layer_kernel(
    sizes, key_lists, live_counts, qkv, grads, out,
    own, left, right, stage, pairs, acc, chain, even, odd, own_grads, left_grads, right_grads, from_next, from_prev, joined,
    lists, chains, tab, links, places, slots, named_here, live_here,
    send, recv, edge_send, edge_recv, back_edge_send, back_edge_recv, back_send, back_recv,
    list_send, list_recv, table_sem,
):
    pairs_total, _, ways = sizes
    heads = own.shape[0]
    z, me = position(sizes)
    x = lax.axis_index("cx")
    wide, slim = 3 * HD, HD
    inner = (z > 0, z < pairs_total - 1)
    kv = pl.ds(HD, 2 * HD)
    own_lists = pltpu.make_async_copy(key_lists, named_here, table_sem.at[0])
    own_counts = pltpu.make_async_copy(live_counts, live_here, table_sem.at[1])
    own_lists.start()
    own_counts.start()
    greet(sizes)

    def piece(h, device, block, t):
        at = device * heads + h
        if t == 3:
            return grads.at[:, pl.ds(pl.multiple_of(at * slim, HD), slim)], own.at[h, rows(block), pl.ds(wide, slim)]
        column = (t + 1) % 3 * HD
        start = pl.multiple_of(at * wide + column, HD)
        return qkv.at[:, pl.ds(start, HD)], own.at[h, rows(block), pl.ds(column, HD)]

    side = z - 1 + 2 * x
    beyond = (side >= 0) & (side < pairs_total)
    list_other = remote(lists.at[x], lists.at[x], list_send.at[0], list_recv.at[0], {"cx": 1 - x})
    list_side = [
        remote(lists.at[x], lists.at[2 + x], list_send.at[1], list_recv.at[1 + x], {"cz": side}),
        remote(lists.at[x], lists.at[2 + x], list_send.at[2], list_recv.at[1 + x], {"cz": side, "cx": 1 - x}),
    ]
    def fetch(h, kinds):
        for t in kinds:
            for k in range(1, ways):
                peer = (me + k) % ways
                src, dst = piece(h, peer, me, t)
                remote(src, dst, send.at[h], recv.at[h, t], peer_id(peer, sizes)).start()
            src, dst = piece(h, me, me, t)
            pltpu.make_async_copy(src, dst, recv.at[h, t]).start()

    own_lists.wait()
    own_counts.wait()
    pack(lists, named_here, live_here, pairs_total, z, x)
    list_other.start()
    pl.when(beyond)(lambda: [c.start() for c in list_side] and None)

    def settled(ref, sem):
        pltpu.make_async_copy(ref, ref, sem).wait()

    def arrived(h, kinds):
        for t in kinds:
            column = 3 * HD if t == 3 else (t + 1) % 3 * HD
            settled(own.at[h, :, pl.ds(column, HD)], recv.at[h, t])

    fetch(0, (0,))
    fetch(0, (1,))

    fetch(1, (0,))
    fetch(1, (1,))
    fetch(0, (2, 3))
    fetch(2, (0,))
    fetch(2, (1,))
    fetch(1, (2, 3))
    fetch(3, (0,))
    fetch(3, (1,))
    fetch(2, (2, 3))
    fetch(3, (2, 3))

    @pl.when(z == 0)
    def _():
        left[...] = jnp.zeros_like(left)
        from_prev[...] = jnp.zeros_like(from_prev)

    @pl.when(z == pairs_total - 1)
    def _():
        right[...] = jnp.zeros_like(right)
        from_next[...] = jnp.zeros_like(from_next)

    chain[0] = jnp.zeros((BLK, 2 * HD), F32)

    list_other_in = remote(lists.at[1 - x], lists.at[1 - x], list_send.at[0], list_recv.at[0], {"cx": 1 - x})
    list_other_in.wait_recv()
    for n, there in ((0, inner[1]), (1, inner[0])):
        come = remote(lists.at[2 + n], lists.at[2 + n], list_send.at[1], list_recv.at[1 + n], {"cx": 1 - x})
        pl.when(there)(come.wait_recv)
    copy = pltpu.make_async_copy(lists, tab, table_sem.at[0])
    copy.start()
    copy.wait()
    tables(tab, places, slots, chains, z)
    copy = pltpu.make_async_copy(chains, links, table_sem.at[1])
    copy.start()
    copy.wait()

    def edge_copies(h, t):
        part = pl.ds(t * HD, HD)
        column = pl.ds((t + 1) * HD, HD)
        up = [
            remote(src, left.at[h, place, part], edge_send.at[h, 0], edge_recv.at[h, 0, t], {"cz": z + 1})
            for n, (src, place) in enumerate(
                ((stage.at[h, 0, :, part], rows(0, NAMED)), (own.at[h, rows(TILES, TILES), column], rows(NAMED, TILES)))
            )
        ]
        down = [
            remote(src, right.at[h, place, part], edge_send.at[h, 1], edge_recv.at[h, 1, t], {"cz": z - 1})
            for n, (src, place) in enumerate(
                ((stage.at[h, 1, :, part], rows(TILES, NAMED)), (own.at[h, rows(0, TILES), column], rows(0, TILES)))
            )
        ]
        return up, down

    def back_edge_copies(h, t):
        part = pl.ds(t * HD, HD)
        up = remote(
            right_grads.at[h, :, part], from_prev.at[h, :, part],
            back_edge_send.at[h, 0], back_edge_recv.at[h, 0, t], {"cz": z + 1},
        )
        down = remote(
            left_grads.at[h, :, part], from_next.at[h, :, part],
            back_edge_send.at[h, 1], back_edge_recv.at[h, 1, t], {"cz": z - 1},
        )
        return [up], [down]

    def start(copies):
        up, down = copies
        pl.when(inner[1])(lambda: [c.start() for c in up] and None)
        pl.when(inner[0])(lambda: [c.start() for c in down] and None)

    def arrive(h, t, refs, sems):
        part = pl.ds(t * HD, HD)
        pl.when(inner[0])(lambda: settled(refs[0].at[h, :, part], sems.at[h, 0, t]))
        pl.when(inner[1])(lambda: settled(refs[1].at[h, :, part], sems.at[h, 1, t]))

    def leave(h, refs, sems):
        pl.when(inner[1])(lambda: settled(refs[0].at[h], sems.at[h, 0]))
        pl.when(inner[0])(lambda: settled(refs[1].at[h], sems.at[h, 1]))

    def edges(h, t):
        arrived(h, (t,))
        columns = slice((t + 1) * HD, (t + 2) * HD)
        for s in range(NAMED):
            for side in range(2):
                chosen = own[h, rows(side * TILES), columns]
                for n in range(1, TILES):
                    chosen = jnp.where(slots[side, s] == n, own[h, rows(side * TILES + n), columns], chosen)
                stage[h, side, rows(s), t * HD : (t + 1) * HD] = chosen
        start(edge_copies(h, t))

    def attend(h, plan=()):
        arrived(h, (2, 3))
        arrive(h, 0, (left, right), edge_recv)
        arrive(h, 1, (left, right), edge_recv)
        pairs[:EDGE] = left[h].reshape(EDGE, BLK, 2 * HD)
        pairs[EDGE : EDGE + PAIR] = own[h, :, HD : 3 * HD].reshape(PAIR, BLK, 2 * HD)
        pairs[EDGE + PAIR :] = right[h].reshape(EDGE, BLK, 2 * HD)
        acc[...] = jnp.zeros_like(acc)

        def operand(i):
            q = own[h, rows(i), :HD]
            g = own[h, rows(i), 3 * HD :]
            zero = jnp.zeros_like(q)
            return jnp.concatenate(
                [jnp.concatenate([q, zero], axis=1), jnp.concatenate([zero, g], axis=1)], axis=0
            )

        def keys(i, columns):
            near = [pairs[EDGE - 1 + i + n, :, columns] for n in range(3)]
            return jnp.concatenate(near + [pairs[places[i, j], :, columns] for j in range(LISTED)], axis=0)

        def issue(i, slot):
            slot[...] = lax.dot_general(
                keys(i, slice(None)), operand(i), (((1,), (1,)), ((), ())), preferred_element_type=F32
            )

        def settle(i, products):
            block = z * PAIR + i
            live = tab[i // TILES, i % TILES, LISTED]
            usable = [block > 0, None, block < pairs_total * PAIR - 1] + [live > j for j in range(LISTED)]
            tiles = [products[n * BLK : (n + 1) * BLK, :HD] for n in range(WIDTH)]
            peaks = [jnp.max(s.reshape(BLK // 8, 8, HD), axis=0) for s in tiles]
            peaks = [s if ok is None else jnp.where(ok, s, -1e30) for s, ok in zip(peaks, usable)]
            top = jnp.max(functools.reduce(jnp.maximum, peaks), axis=0, keepdims=True)
            tops = [top if ok is None else jnp.where(ok, top, 1e30) for ok in usable]
            powers = jnp.concatenate([jnp.exp2((s - b) * RATE) for s, b in zip(tiles, tops)], axis=0)
            dp = products[:, HD:]
            over = 1.0 / jnp.sum(powers, axis=0, keepdims=True)
            soft = powers * over
            ds = soft * (dp - jnp.sum(powers * dp, axis=0, keepdims=True) * over)
            ds_low = ds.astype(BF16)
            low = jnp.concatenate([ds_low, soft.astype(BF16)], axis=1)
            terms = jnp.dot(low, operand(i), preferred_element_type=F32)
            grad_q = lax.dot_general(
                ds_low, keys(i, slice(0, HD)), (((0,), (0,)), ((), ())), preferred_element_type=F32
            )
            joined[h, rows(i), :HD] = (grad_q * SCALE).astype(BF16)
            acc[rows(EDGE - 1 + i, 3), :] += terms[: 3 * BLK]
            for j in range(LISTED):
                n = i * LISTED + j
                chain[n + 1] = terms[(3 + j) * BLK : (4 + j) * BLK] + chain[links[0, n]]

        def step(n, carry):
            i = 2 * n
            for when, task in plan:
                pl.when(n == when)(task)
            issue(i + 1, odd)
            settle(i, even)
            issue((i + 2) % PAIR, even)
            settle(i + 1, odd)
            return carry

        issue(0, even)
        lax.fori_loop(0, PAIR // 2, step, 0)

        def total(p):
            value = acc[rows(p), :] + chain[links[1, p]]
            return jnp.concatenate([value[:, :HD] * SCALE, value[:, HD:]], axis=1)

        def edge_total(p, carry):
            left_grads[h, rows(p), :] = total(p).astype(BF16)
            right_grads[h, rows(p), :] = total(EDGE + PAIR + p).astype(BF16)
            return carry

        def own_total(p, carry):
            own_grads[h, rows(p), :] = total(EDGE + p)
            return carry

        lax.fori_loop(0, EDGE, edge_total, 0)
        start(back_edge_copies(h, 0))
        start(back_edge_copies(h, 1))
        lax.fori_loop(0, PAIR, own_total, 0)

    parts = [slice(t * HD, (t + 1) * HD) for t in range(3)]

    def column(device, h, t):
        return out.at[:, pl.ds(pl.multiple_of((device * heads + h) * wide + t * HD, HD), HD)]

    def give_copy(h, t, k):
        peer = (me + k) % ways
        return remote(
            joined.at[h, rows(peer), parts[t]], column(me, h, t), back_send.at[h], back_recv.at[h],
            peer_id(peer, sizes),
        )

    def give_local(h, t):
        return pltpu.make_async_copy(joined.at[h, rows(me), parts[t]], column(me, h, t), back_recv.at[h])

    def give(h, t):
        for k in range(1, ways):
            give_copy(h, t, k).start()
        give_local(h, t).start()

    def combine(h, part):
        arrive(h, part, (from_prev, from_next), back_edge_recv)
        columns = parts[part]
        for t in range(PAIR):
            value = own_grads[h, rows(t), columns]
            if t < TILES:
                near, far, table, base = from_prev, from_next, 0, t
                near_at, far_at = t, 0
            else:
                near, far, table, base = from_next, from_prev, 1, t - TILES
                near_at, far_at = NAMED + t - TILES, TILES
            value += near[h, rows(near_at), columns].astype(F32)
            for s in range(NAMED):
                term = far[h, rows(far_at + s), columns].astype(F32)
                value += jnp.where(slots[table, s] == base, term, 0.0)
            joined[h, rows(t), parts[part + 1]] = value.astype(BF16)
        give(h, part + 1)

    edges(0, 0)
    edges(0, 1)
    edges(1, 0)
    edges(1, 1)
    attend(0, [(2, functools.partial(edges, 2, 0)), (2, functools.partial(edges, 2, 1))])
    give(0, 0)
    attend(1, [(2, functools.partial(edges, 3, 0)), (2, functools.partial(edges, 3, 1))])
    give(1, 0)
    combine(0, 0)
    combine(0, 1)
    attend(2)
    give(2, 0)
    attend(3)
    give(3, 0)
    combine(1, 0)
    combine(1, 1)
    combine(2, 0)
    combine(2, 1)
    combine(3, 0)
    combine(3, 1)

    for h in range(heads):
        settled(own.at[h, pl.ds(0, (ways - 1) * BLK)], send.at[h])
        leave(h, (left, right), edge_send)
        leave(h, (right_grads, left_grads), back_edge_send)
        settled(joined.at[h, pl.ds(0, (ways - 1) * BLK)], back_send.at[h])
        settled(out.at[:, pl.ds(0, ways * wide)], back_recv.at[h])
    list_other.wait_send()
    pl.when(beyond)(lambda: [c.wait_send() for c in list_side] and None)


def shards(qkv, grad_out, key_lists, live_counts):
    heads_total = lax.axis_size("head")
    ways = lax.axis_size("cx") * heads_total
    sizes = (lax.axis_size("cz"), heads_total, ways)
    heads = qkv.shape[1] // (3 * HD) // ways
    full = qkv.shape[0] * ways
    hbm = pl.BlockSpec(memory_space=pltpu.HBM)
    dma = pltpu.SemaphoreType.DMA
    edge = pltpu.VMEM((heads, EDGE * BLK, 2 * HD), BF16)
    return pl.pallas_call(
        functools.partial(layer_kernel, sizes),
        in_specs=[hbm] * 4,
        out_specs=pl.BlockSpec(memory_space=pltpu.VMEM),
        out_shape=pltpu.VMEM(qkv.shape, BF16),
        scratch_shapes=[
            pltpu.VMEM((heads, full, 4 * HD), BF16), edge, edge,
            pltpu.VMEM((heads, 2, NAMED * BLK, 2 * HD), BF16),
            pltpu.VMEM((ALL, BLK, 2 * HD), BF16),
            pltpu.VMEM((ALL * BLK, 2 * HD), F32),
            pltpu.VMEM((PAIR * LISTED + 1, BLK, 2 * HD), F32),
            pltpu.VMEM((WIDTH * BLK, 2 * HD), F32), pltpu.VMEM((WIDTH * BLK, 2 * HD), F32),
            pltpu.VMEM((heads, full, 2 * HD), F32),
            edge, edge, edge, edge,
            pltpu.VMEM((heads, full, 3 * HD), BF16),
            pltpu.VMEM((4, 8, 128), I32), pltpu.VMEM((8, 128), I32),
            pltpu.SMEM((4, 8, 128), I32), pltpu.SMEM((8, 128), I32),
            pltpu.SMEM((PAIR, LISTED), I32), pltpu.SMEM((2, NAMED), I32),
            pltpu.SMEM((TILES, LISTED), I32), pltpu.SMEM((TILES,), I32),
            dma((heads,)), dma((heads, 4)),
            dma((heads, 2)), dma((heads, 2, 2)), dma((heads, 2)), dma((heads, 2, 2)),
            dma((heads,)), dma((heads,)),
            dma((3,)), dma((3,)), dma((2,)),
        ],
        compiler_params=pltpu.CompilerParams(
            collective_id=0, has_side_effects=True, vmem_limit_bytes=60_000_000
        ),
        name="layer",
    )(key_lists, live_counts, qkv, grad_out)


def solution(mesh):
    ctx, head = mesh.shape["ctx"], mesh.shape["head"]
    split = Mesh(mesh.devices.reshape(ctx // 2, 2, head), ("cz", "cx", "head"))
    both = ("cz", "cx")
    tokens = P((*both, "head"), None)
    return jax.shard_map(
        shards, mesh=split, in_specs=(tokens, tokens, P(both, None), P(both)), out_specs=tokens, check_vma=False
    )
```

```python
import functools

import jax
import jax.numpy as jnp
from jax import lax
from jax.experimental import pallas as pl
from jax.experimental.pallas import tpu as pltpu
from jax.sharding import Mesh, PartitionSpec as P

HD = 128
BLK = 128
TILES = 4
LISTED = 4
CUTS = 2
NAMED = 2
PAIR = 2 * TILES
EDGE = NAMED + TILES
ALL = 2 * EDGE + PAIR
WIDTH = 3 + LISTED
SCALE = HD ** (-0.5)
RATE = SCALE * 1.4426950408889634
MESH = pl.DeviceIdType.MESH
I32 = jnp.int32
F32 = jnp.float32
BF16 = jnp.bfloat16


def rows(block, count=1):
    start = block * BLK
    return pl.ds(start if isinstance(start, int) else pl.multiple_of(start, BLK), count * BLK)


def position(sizes):
    pairs_total, heads_total, ways = sizes
    z = lax.axis_index("cz")
    me = lax.axis_index("cx") * heads_total + lax.axis_index("head")
    return z, me


def peer_id(peer, sizes):
    return {"cx": peer // sizes[1], "head": peer % sizes[1]}


def greet(sizes):
    pairs_total, _, ways = sizes
    z, me = position(sizes)
    x = lax.axis_index("cx")
    side = z - 1 + 2 * x
    inside = (side >= 0) & (side < pairs_total)
    barrier = pltpu.get_barrier_semaphore()

    def signal(device_id):
        pl.semaphore_signal(barrier, inc=1, device_id=device_id, device_id_type=MESH)

    for k in range(1, ways):
        signal(peer_id((me + k) % ways, sizes))
    pl.when(z > 0)(lambda: signal({"cz": z - 1}))
    pl.when(z < pairs_total - 1)(lambda: signal({"cz": z + 1}))
    pl.when(inside)(lambda: signal({"cz": side, "cx": 1 - x}))
    neighbours = jnp.minimum(z, 1) + jnp.minimum(pairs_total - 1 - z, 1) + jnp.where(inside, 1, 0)
    pl.semaphore_wait(barrier, ways - 1 + neighbours)


def remote(src, dst, send, recv, device_id):
    return pltpu.make_async_remote_copy(
        src_ref=src, dst_ref=dst, send_sem=send, recv_sem=recv, device_id=device_id, device_id_type=MESH
    )


def pack(lists, key_lists, live_counts, pairs_total, z, x):
    row = lax.broadcasted_iota(I32, (8, 128), 0)
    col = lax.broadcasted_iota(I32, (8, 128), 1)
    value = jnp.full((8, 128), -1, I32)
    for b in range(TILES):
        for j in range(LISTED):
            value = jnp.where((row == b) & (col == j), key_lists[b, j], value)
        value = jnp.where((row == b) & (col == LISTED), live_counts[b], value)
    lists[x] = value

    @pl.when(z == pairs_total - 1)
    def _():
        lists[2] = jnp.full((8, 128), -1, I32)

    @pl.when(z == 0)
    def _():
        lists[3] = jnp.full((8, 128), -1, I32)


def tables(tab, places, slots, chains, z):
    base = z * PAIR

    def named(run, first):
        flags = [jnp.int32(0)] * TILES
        for b in range(TILES):
            for j in range(LISTED):
                at = tab[run, b, j] - first
                flags = [jnp.where(at == t, 1, flag) for t, flag in enumerate(flags)]
        ranks = [jnp.int32(0)]
        for flag in flags[:-1]:
            ranks.append(ranks[-1] + flag)
        return flags, ranks

    for side, (run, first) in enumerate(((2, base), (3, base + TILES))):
        flags, ranks = named(run, first)
        for s in range(NAMED):
            chosen = jnp.int32(0)
            for t in range(TILES):
                chosen = jnp.where((flags[t] == 1) & (ranks[t] == s), t, chosen)
            slots[side, s] = chosen
    row = lax.broadcasted_iota(I32, (8, 128), 0)
    col = lax.broadcasted_iota(I32, (8, 128), 1)
    before = jnp.zeros((8, 128), I32)
    last = jnp.zeros((8, 128), I32)
    along = jnp.full((8, 128), -1, I32)
    found = []
    for run, (first, start) in enumerate(((base - PAIR, 0), (base + PAIR + TILES, EDGE + PAIR + TILES))):
        _, ranks = named(run, first)
        for b in range(TILES):
            for j in range(LISTED):
                block = tab[run, b, j]
                far = jnp.int32(0)
                for t in range(1, TILES):
                    far = jnp.where(block - first == t, ranks[t], far)
                outside = (block < base - TILES) if run == 0 else (block >= base + PAIR + TILES)
                place = jnp.where(outside, start + far, EDGE + block - base)
                place = jnp.clip(place, 0, ALL - 1)
                places[run * TILES + b, j] = place
                found.append(place)
    for n, place in enumerate(found):
        along = jnp.where(col == n, place, along)
    for n, place in enumerate(found):
        before = jnp.where((along == place) & (col > n), n + 1, before)
        last = jnp.where(col == place, n + 1, last)
    chains[...] = jnp.where(row == 0, before, last)


def layer_kernel(
    sizes, key_lists, live_counts, qkv, grads, out,
    own, left, right, stage, pairs, acc, chain, even, odd, own_grads, left_grads, right_grads, from_next, from_prev, joined,
    lists, chains, tab, links, places, slots, named_here, live_here,
    send, recv, edge_send, edge_recv, back_edge_send, back_edge_recv, back_send, back_recv,
    list_send, list_recv, table_sem,
):
    pairs_total, _, ways = sizes
    heads = own.shape[0]
    z, me = position(sizes)
    x = lax.axis_index("cx")
    wide, slim = 3 * HD, HD
    inner = (z > 0, z < pairs_total - 1)
    kv = pl.ds(HD, 2 * HD)
    own_lists = pltpu.make_async_copy(key_lists, named_here, table_sem.at[0])
    own_counts = pltpu.make_async_copy(live_counts, live_here, table_sem.at[1])
    own_lists.start()
    own_counts.start()
    greet(sizes)

    def piece(h, device, block, t):
        at = device * heads + h
        if t == 3:
            return grads.at[:, pl.ds(pl.multiple_of(at * slim, HD), slim)], own.at[h, rows(block), pl.ds(wide, slim)]
        column = (t + 1) % 3 * HD
        start = pl.multiple_of(at * wide + column, HD)
        return qkv.at[:, pl.ds(start, HD)], own.at[h, rows(block), pl.ds(column, HD)]

    side = z - 1 + 2 * x
    beyond = (side >= 0) & (side < pairs_total)
    list_other = remote(lists.at[x], lists.at[x], list_send.at[0], list_recv.at[0], {"cx": 1 - x})
    list_side = [
        remote(lists.at[x], lists.at[2 + x], list_send.at[1], list_recv.at[1 + x], {"cz": side}),
        remote(lists.at[x], lists.at[2 + x], list_send.at[2], list_recv.at[1 + x], {"cz": side, "cx": 1 - x}),
    ]
    def fetch(h, kinds):
        for t in kinds:
            for part in range(CUTS):
                few = pl.ds(part * (BLK // CUTS), BLK // CUTS)
                for k in range(1, ways):
                    peer = (me + k) % ways
                    src, dst = piece(h, peer, me, t)
                    remote(src.at[few], dst.at[few], send.at[h], recv.at[h, t], peer_id(peer, sizes)).start()
            src, dst = piece(h, me, me, t)
            pltpu.make_async_copy(src, dst, recv.at[h, t]).start()

    own_lists.wait()
    own_counts.wait()
    pack(lists, named_here, live_here, pairs_total, z, x)
    list_other.start()
    pl.when(beyond)(lambda: [c.start() for c in list_side] and None)

    def settled(ref, sem):
        pltpu.make_async_copy(ref, ref, sem).wait()

    def arrived(h, kinds):
        for t in kinds:
            column = 3 * HD if t == 3 else (t + 1) % 3 * HD
            settled(own.at[h, :, pl.ds(column, HD)], recv.at[h, t])

    fetch(0, (0,))
    fetch(0, (1,))

    fetch(1, (0,))
    fetch(1, (1,))
    fetch(0, (2, 3))
    fetch(2, (0,))
    fetch(2, (1,))
    fetch(1, (2, 3))
    fetch(3, (0,))
    fetch(3, (1,))
    fetch(2, (2, 3))
    fetch(3, (2, 3))

    @pl.when(z == 0)
    def _():
        left[...] = jnp.zeros_like(left)
        from_prev[...] = jnp.zeros_like(from_prev)

    @pl.when(z == pairs_total - 1)
    def _():
        right[...] = jnp.zeros_like(right)
        from_next[...] = jnp.zeros_like(from_next)

    chain[0] = jnp.zeros((BLK, 2 * HD), F32)

    list_other_in = remote(lists.at[1 - x], lists.at[1 - x], list_send.at[0], list_recv.at[0], {"cx": 1 - x})
    list_other_in.wait_recv()
    for n, there in ((0, inner[1]), (1, inner[0])):
        come = remote(lists.at[2 + n], lists.at[2 + n], list_send.at[1], list_recv.at[1 + n], {"cx": 1 - x})
        pl.when(there)(come.wait_recv)
    copy = pltpu.make_async_copy(lists, tab, table_sem.at[0])
    copy.start()
    copy.wait()
    tables(tab, places, slots, chains, z)
    copy = pltpu.make_async_copy(chains, links, table_sem.at[1])
    copy.start()
    copy.wait()

    def edge_copies(h, t):
        part = pl.ds(t * HD, HD)
        column = pl.ds((t + 1) * HD, HD)
        up = [
            remote(src, left.at[h, place, part], edge_send.at[h, 0], edge_recv.at[h, 0, t], {"cz": z + 1})
            for n, (src, place) in enumerate(
                ((stage.at[h, 0, :, part], rows(0, NAMED)), (own.at[h, rows(TILES, TILES), column], rows(NAMED, TILES)))
            )
        ]
        down = [
            remote(src, right.at[h, place, part], edge_send.at[h, 1], edge_recv.at[h, 1, t], {"cz": z - 1})
            for n, (src, place) in enumerate(
                ((stage.at[h, 1, :, part], rows(TILES, NAMED)), (own.at[h, rows(0, TILES), column], rows(0, TILES)))
            )
        ]
        return up, down

    def back_edge_copies(h, t):
        part = pl.ds(t * HD, HD)
        up = remote(
            right_grads.at[h, :, part], from_prev.at[h, :, part],
            back_edge_send.at[h, 0], back_edge_recv.at[h, 0, t], {"cz": z + 1},
        )
        down = remote(
            left_grads.at[h, :, part], from_next.at[h, :, part],
            back_edge_send.at[h, 1], back_edge_recv.at[h, 1, t], {"cz": z - 1},
        )
        return [up], [down]

    def start(copies):
        up, down = copies
        pl.when(inner[1])(lambda: [c.start() for c in up] and None)
        pl.when(inner[0])(lambda: [c.start() for c in down] and None)

    def arrive(h, t, refs, sems):
        part = pl.ds(t * HD, HD)
        pl.when(inner[0])(lambda: settled(refs[0].at[h, :, part], sems.at[h, 0, t]))
        pl.when(inner[1])(lambda: settled(refs[1].at[h, :, part], sems.at[h, 1, t]))

    def leave(h, refs, sems):
        pl.when(inner[1])(lambda: settled(refs[0].at[h], sems.at[h, 0]))
        pl.when(inner[0])(lambda: settled(refs[1].at[h], sems.at[h, 1]))

    def edges(h, t):
        arrived(h, (t,))
        columns = slice((t + 1) * HD, (t + 2) * HD)
        for s in range(NAMED):
            for side in range(2):
                chosen = own[h, rows(side * TILES), columns]
                for n in range(1, TILES):
                    chosen = jnp.where(slots[side, s] == n, own[h, rows(side * TILES + n), columns], chosen)
                stage[h, side, rows(s), t * HD : (t + 1) * HD] = chosen
        start(edge_copies(h, t))

    def attend(h, plan=()):
        arrived(h, (2, 3))
        arrive(h, 0, (left, right), edge_recv)
        arrive(h, 1, (left, right), edge_recv)
        pairs[:EDGE] = left[h].reshape(EDGE, BLK, 2 * HD)
        pairs[EDGE : EDGE + PAIR] = own[h, :, HD : 3 * HD].reshape(PAIR, BLK, 2 * HD)
        pairs[EDGE + PAIR :] = right[h].reshape(EDGE, BLK, 2 * HD)
        acc[...] = jnp.zeros_like(acc)

        def operand(i):
            q = own[h, rows(i), :HD]
            g = own[h, rows(i), 3 * HD :]
            zero = jnp.zeros_like(q)
            return jnp.concatenate(
                [jnp.concatenate([q, zero], axis=1), jnp.concatenate([zero, g], axis=1)], axis=0
            )

        def keys(i, columns):
            near = [pairs[EDGE - 1 + i + n, :, columns] for n in range(3)]
            return jnp.concatenate(near + [pairs[places[i, j], :, columns] for j in range(LISTED)], axis=0)

        def issue(i, slot):
            slot[...] = lax.dot_general(
                keys(i, slice(None)), operand(i), (((1,), (1,)), ((), ())), preferred_element_type=F32
            )

        def settle(i, products):
            block = z * PAIR + i
            live = tab[i // TILES, i % TILES, LISTED]
            usable = [block > 0, None, block < pairs_total * PAIR - 1] + [live > j for j in range(LISTED)]
            tiles = [products[n * BLK : (n + 1) * BLK, :HD] for n in range(WIDTH)]
            peaks = [jnp.max(s.reshape(BLK // 8, 8, HD), axis=0) for s in tiles]
            peaks = [s if ok is None else jnp.where(ok, s, -1e30) for s, ok in zip(peaks, usable)]
            top = jnp.max(functools.reduce(jnp.maximum, peaks), axis=0, keepdims=True)
            tops = [top if ok is None else jnp.where(ok, top, 1e30) for ok in usable]
            powers = jnp.concatenate([jnp.exp2((s - b) * RATE) for s, b in zip(tiles, tops)], axis=0)
            dp = products[:, HD:]
            over = 1.0 / jnp.sum(powers, axis=0, keepdims=True)
            soft = powers * over
            ds = soft * (dp - jnp.sum(powers * dp, axis=0, keepdims=True) * over)
            ds_low = ds.astype(BF16)
            low = jnp.concatenate([ds_low, soft.astype(BF16)], axis=1)
            terms = jnp.dot(low, operand(i), preferred_element_type=F32)
            grad_q = lax.dot_general(
                ds_low, keys(i, slice(0, HD)), (((0,), (0,)), ((), ())), preferred_element_type=F32
            )
            joined[h, rows(i), :HD] = (grad_q * SCALE).astype(BF16)
            acc[rows(EDGE - 1 + i, 3), :] += terms[: 3 * BLK]
            for j in range(LISTED):
                n = i * LISTED + j
                chain[n + 1] = terms[(3 + j) * BLK : (4 + j) * BLK] + chain[links[0, n]]

        def step(n, carry):
            i = 2 * n
            for when, task in plan:
                pl.when(n == when)(task)
            issue(i + 1, odd)
            settle(i, even)
            issue((i + 2) % PAIR, even)
            settle(i + 1, odd)
            return carry

        issue(0, even)
        lax.fori_loop(0, PAIR // 2, step, 0)

        def total(p):
            value = acc[rows(p), :] + chain[links[1, p]]
            return jnp.concatenate([value[:, :HD] * SCALE, value[:, HD:]], axis=1)

        def edge_total(p, carry):
            left_grads[h, rows(p), :] = total(p).astype(BF16)
            right_grads[h, rows(p), :] = total(EDGE + PAIR + p).astype(BF16)
            return carry

        def own_total(p, carry):
            own_grads[h, rows(p), :] = total(EDGE + p)
            return carry

        lax.fori_loop(0, EDGE, edge_total, 0)
        start(back_edge_copies(h, 0))
        start(back_edge_copies(h, 1))
        lax.fori_loop(0, PAIR, own_total, 0)

    parts = [slice(t * HD, (t + 1) * HD) for t in range(3)]

    def column(device, h, t):
        return out.at[:, pl.ds(pl.multiple_of((device * heads + h) * wide + t * HD, HD), HD)]

    def give_copy(h, t, k):
        peer = (me + k) % ways
        return remote(
            joined.at[h, rows(peer), parts[t]], column(me, h, t), back_send.at[h], back_recv.at[h],
            peer_id(peer, sizes),
        )

    def give_local(h, t):
        return pltpu.make_async_copy(joined.at[h, rows(me), parts[t]], column(me, h, t), back_recv.at[h])

    def give(h, t):
        for k in range(1, ways):
            give_copy(h, t, k).start()
        give_local(h, t).start()

    def combine(h, part):
        arrive(h, part, (from_prev, from_next), back_edge_recv)
        columns = parts[part]
        for t in range(PAIR):
            value = own_grads[h, rows(t), columns]
            if t < TILES:
                near, far, table, base = from_prev, from_next, 0, t
                near_at, far_at = t, 0
            else:
                near, far, table, base = from_next, from_prev, 1, t - TILES
                near_at, far_at = NAMED + t - TILES, TILES
            value += near[h, rows(near_at), columns].astype(F32)
            for s in range(NAMED):
                term = far[h, rows(far_at + s), columns].astype(F32)
                value += jnp.where(slots[table, s] == base, term, 0.0)
            joined[h, rows(t), parts[part + 1]] = value.astype(BF16)
        give(h, part + 1)

    edges(0, 0)
    edges(0, 1)
    edges(1, 0)
    edges(1, 1)
    attend(0, [(2, functools.partial(edges, 2, 0)), (2, functools.partial(edges, 2, 1))])
    give(0, 0)
    attend(1, [(2, functools.partial(edges, 3, 0)), (2, functools.partial(edges, 3, 1))])
    give(1, 0)
    combine(0, 0)
    combine(0, 1)
    attend(2)
    give(2, 0)
    attend(3)
    give(3, 0)
    combine(1, 0)
    combine(1, 1)
    combine(2, 0)
    combine(2, 1)
    combine(3, 0)
    combine(3, 1)

    for h in range(heads):
        settled(own.at[h, pl.ds(0, (ways - 1) * BLK)], send.at[h])
        leave(h, (left, right), edge_send)
        leave(h, (right_grads, left_grads), back_edge_send)
        settled(joined.at[h, pl.ds(0, (ways - 1) * BLK)], back_send.at[h])
        settled(out.at[:, pl.ds(0, ways * wide)], back_recv.at[h])
    list_other.wait_send()
    pl.when(beyond)(lambda: [c.wait_send() for c in list_side] and None)


def shards(qkv, grad_out, key_lists, live_counts):
    heads_total = lax.axis_size("head")
    ways = lax.axis_size("cx") * heads_total
    sizes = (lax.axis_size("cz"), heads_total, ways)
    heads = qkv.shape[1] // (3 * HD) // ways
    full = qkv.shape[0] * ways
    hbm = pl.BlockSpec(memory_space=pltpu.HBM)
    dma = pltpu.SemaphoreType.DMA
    edge = pltpu.VMEM((heads, EDGE * BLK, 2 * HD), BF16)
    return pl.pallas_call(
        functools.partial(layer_kernel, sizes),
        in_specs=[hbm] * 4,
        out_specs=pl.BlockSpec(memory_space=pltpu.VMEM),
        out_shape=pltpu.VMEM(qkv.shape, BF16),
        scratch_shapes=[
            pltpu.VMEM((heads, full, 4 * HD), BF16), edge, edge,
            pltpu.VMEM((heads, 2, NAMED * BLK, 2 * HD), BF16),
            pltpu.VMEM((ALL, BLK, 2 * HD), BF16),
            pltpu.VMEM((ALL * BLK, 2 * HD), F32),
            pltpu.VMEM((PAIR * LISTED + 1, BLK, 2 * HD), F32),
            pltpu.VMEM((WIDTH * BLK, 2 * HD), F32), pltpu.VMEM((WIDTH * BLK, 2 * HD), F32),
            pltpu.VMEM((heads, full, 2 * HD), F32),
            edge, edge, edge, edge,
            pltpu.VMEM((heads, full, 3 * HD), BF16),
            pltpu.VMEM((4, 8, 128), I32), pltpu.VMEM((8, 128), I32),
            pltpu.SMEM((4, 8, 128), I32), pltpu.SMEM((8, 128), I32),
            pltpu.SMEM((PAIR, LISTED), I32), pltpu.SMEM((2, NAMED), I32),
            pltpu.SMEM((TILES, LISTED), I32), pltpu.SMEM((TILES,), I32),
            dma((heads,)), dma((heads, 4)),
            dma((heads, 2)), dma((heads, 2, 2)), dma((heads, 2)), dma((heads, 2, 2)),
            dma((heads,)), dma((heads,)),
            dma((3,)), dma((3,)), dma((2,)),
        ],
        compiler_params=pltpu.CompilerParams(
            collective_id=0, has_side_effects=True, vmem_limit_bytes=60_000_000
        ),
        name="layer",
    )(key_lists, live_counts, qkv, grad_out)


def solution(mesh):
    ctx, head = mesh.shape["ctx"], mesh.shape["head"]
    split = Mesh(mesh.devices.reshape(ctx // 2, 2, head), ("cz", "cx", "head"))
    both = ("cz", "cx")
    tokens = P((*both, "head"), None)
    return jax.shard_map(
        shards, mesh=split, in_specs=(tokens, tokens, P(both, None), P(both)), out_specs=tokens, check_vma=False
    )
```
